256 devices in a mesh: dp: 64 (over x, y, z_hi), tensor: 4 (over z_lo, core).
Axes of the slice: x: 4, y: 4, z: 8 (z_hi: 4, z_lo: 2; z = z_hi * 2 + z_lo), core: 2. Of those that a mesh axis runs over, the one named last changes fastest.
Arguments:
- tokens: bfloat16 [32768, 6144], P('dp', 'tensor'), may hold values from -6 to 6
- block_mask: int32 [128, 4, 4], P('dp'), may hold values from 0 to 1
- norm_gain: float32 [6144], replicated, may hold values from 0.25 to 1.75
- w_query: bfloat16 [6144, 3072], P('dp', 'tensor'), may hold values from -0.078125 to 0.078125
- w_key: bfloat16 [6144, 3072], P('dp', 'tensor'), may hold values from -0.078125 to 0.078125
- w_value: bfloat16 [6144, 3072], P('dp', 'tensor'), may hold values from -0.078125 to 0.078125
- query_gain: float32 [128], replicated, may hold values from 0.1 to 1.9
- key_gain: float32 [128], replicated, may hold values from 0.1 to 1.9
Outputs:
- attended: bfloat16 [32768, 3072], P('dp', 'tensor')
The draws below stay inside these ranges and needn't reach their ends.
All inputs are finite; a program needn't handle non-finite values.
Results may differ from the reference program's by a relative error of at most 0.0085.
Values may be sent and summed in bfloat16 or wider, within the bound.
A program may use at most 192 MiB of HBM per device.

```python
import jax
import jax.numpy as jnp
from jax import lax

D = 6144
DH = 128
HEADS = 24
TPD = 256
BLOCK = 64
NBLK = 4
HD = 3072
DRAWS = 128
TOKENS = 32768


def place_ends(entries, key, least, top_value):
    spot = [jax.random.randint(jax.random.fold_in(key, axis), (), 0, length) for axis, length in enumerate(entries.shape)]
    longest = entries.shape.index(max(entries.shape))
    beside = spot[:longest] + [(spot[longest] + 1) % entries.shape[longest]] + spot[longest + 1:]
    return entries.at[tuple(spot)].set(least).at[tuple(beside)].set(top_value)


def steps_of(own_key, dims, cuts, smallest, high):
    level = 1.0
    for dim, blocks in cuts:
        heights = jax.random.uniform(jax.random.fold_in(jax.random.fold_in(own_key, 6), dim), (blocks,), jnp.float32, smallest / len(cuts), high / len(cuts))
        level = level * jnp.repeat(jnp.exp(heights), dims[dim] // blocks).reshape((-1,) + (1,) * (len(dims) - 1 - dim))
    return level


def gaussian(stream_key, extent, scale, most, shards=(), held_as=jnp.bfloat16):
    values = scale * jax.random.normal(stream_key, extent, jnp.float32)
    if shards:
        values = values * steps_of(stream_key, extent, shards, -0.22, 0.18)
    return jnp.clip(values, -most, most).astype(held_as)


def setup_inputs(seed: int = 0) -> dict:
    seeds = jax.random.split(jax.random.key(seed), 9)
    tokens = gaussian(seeds[0], (TOKENS, D), 1.0, 6.0, ((0, 64), (1, 4)))
    block_mask = place_ends(jax.random.randint(seeds[1], (DRAWS, NBLK, NBLK), 0, 2), jax.random.fold_in(seeds[1], 1), 0, 1).astype(jnp.int32)
    norm_gain = jnp.clip(1.0 + 0.15 * jax.random.normal(seeds[2], (D,), jnp.float32), 0.25, 1.75)
    w_query = gaussian(seeds[3], (D, HD), D ** -0.5, 0.078125, ((0, 64), (1, 4)))
    w_key = gaussian(seeds[4], (D, HD), D ** -0.5, 0.078125, ((0, 64), (1, 4)))
    w_value = gaussian(seeds[5], (D, HD), D ** -0.5, 0.078125, ((0, 64), (1, 4)))
    query_gain = jnp.clip(1.0 + 0.18 * jax.random.normal(seeds[6], (DH,), jnp.float32), 0.1, 1.9)
    key_gain = jnp.clip(1.0 + 0.18 * jax.random.normal(seeds[7], (DH,), jnp.float32), 0.1, 1.9)
    return dict(tokens=tokens, block_mask=block_mask, norm_gain=norm_gain, w_query=w_query, w_key=w_key, w_value=w_value, query_gain=query_gain, key_gain=key_gain)


EPS = 1e-06

def layer_norm(rows, gain):
    values = rows.astype(jnp.float32)
    mean = lax.optimization_barrier(jnp.mean(values, axis=-1, keepdims=True))
    mean_sq = lax.optimization_barrier(jnp.mean(values * values, axis=-1, keepdims=True))
    return (values - mean) * lax.rsqrt(mean_sq - mean * mean + EPS) * gain

def head_norm(values, gain):
    mean_sq = lax.optimization_barrier(jnp.mean(values * values, axis=-1, keepdims=True))
    return values * lax.rsqrt(mean_sq + EPS) * gain

def expand_mask(block_mask):
    blocks = block_mask.shape[-1]
    allowed = (block_mask > 0) | (jnp.arange(blocks)[:, None] == jnp.arange(blocks)[None, :])
    allowed = jnp.repeat(jnp.repeat(allowed, BLOCK, axis=-2), BLOCK, axis=-1)
    return allowed

def reference(tokens, block_mask, norm_gain, w_query, w_key, w_value, query_gain, key_gain):
    normed = layer_norm(tokens, norm_gain).astype(jnp.bfloat16)
    query = jnp.dot(normed, w_query, preferred_element_type=jnp.float32)
    key = jnp.dot(normed, w_key, preferred_element_type=jnp.float32)
    value = jnp.dot(normed, w_value, preferred_element_type=jnp.float32).astype(jnp.bfloat16)
    query_n = head_norm(query.reshape(DRAWS, TPD, HEADS, DH), query_gain).astype(jnp.bfloat16)
    key_n = head_norm(key.reshape(DRAWS, TPD, HEADS, DH), key_gain).astype(jnp.bfloat16)
    value = value.reshape(DRAWS, TPD, HEADS, DH)

    def one_draw(items):
        qd, kd, vd, md = items
        scores = jnp.einsum('qhe,khe->hqk', qd.astype(jnp.float32), kd.astype(jnp.float32)) / jnp.sqrt(jnp.float32(DH))
        allowed = expand_mask(md)
        scores = jnp.where(allowed[None], scores, jnp.float32(-1e+30))
        top = lax.optimization_barrier(jnp.max(scores, axis=-1, keepdims=True))
        weights = jnp.exp(scores - top)
        probs = (weights / lax.optimization_barrier(jnp.sum(weights, axis=-1, keepdims=True))).astype(jnp.bfloat16)
        out = jnp.einsum('hqk,khe->qhe', probs.astype(jnp.float32), vd.astype(jnp.float32))
        return out.astype(jnp.bfloat16).reshape(TPD, HD)
    result = lax.map(one_draw, (query_n, key_n, value, block_mask))
    return result.reshape(TOKENS, HD)
```

```python
import jax
import jax.numpy as jnp
from jax import lax
from jax.experimental import pallas as pl
from jax.experimental.pallas import tpu as pltpu
from jax.sharding import PartitionSpec as P

DH = 128
TPD = 256
BLOCK = 64
EPS = 1e-06
MESH = pl.DeviceIdType.MESH

ROWS = 96
FEAT = 1536
D = 6144
NC = 384
N = 3 * NC

AXP, AXM, AZ = 0, 2, 4
AD, AL, AOP, AOM = 6, 7, 8, 9
AIIP, AIIM, AIII = 10, 12, 14
MK = 16
SW = 19
ZP, ZM, ZFP, ZFM = 21, 23, 25, 26
YP, YM = 27, 35
YFP, YFM = 43, 47
DO = 51
DYM, DYP, DYO = 59, 61, 63
OUT = 65
COUNT = 69


def kernel(tok, mk, gn, wq, wk, wv, qg, kg, out, a_buf, b_buf, ws, acc, s1, s2, cs, mbuf, obuf, ssem, rsem):
    dp = lax.axis_index("dp")
    t = lax.axis_index("tensor")
    x, y, zh = dp // 16, (dp // 4) % 4, dp % 4
    zlo, c = t // 2, t % 2
    xp, xm, xo = (x + 1) % 4, (x + 3) % 4, (x + 2) % 4
    yp, ym, yo = (y + 1) % 4, (y + 3) % 4, (y + 2) % 4
    zp, zm, zo = (zh + 1) % 4, (zh + 3) % 4, (zh + 2) % 4

    def dev(x_=None, y_=None, zh_=None, zlo_=None, c_=None):
        x_ = x if x_ is None else x_
        y_ = y if y_ is None else y_
        zh_ = zh if zh_ is None else zh_
        zlo_ = zlo if zlo_ is None else zlo_
        c_ = c if c_ is None else c_
        return (x_ * 16 + y_ * 4 + zh_, zlo_ * 2 + c_)

    def remote(src, dst, sid, rid, device):
        return pltpu.make_async_remote_copy(
            src_ref=src, dst_ref=dst, send_sem=ssem.at[sid], recv_sem=rsem.at[rid], device_id=device, device_id_type=MESH
        )

    def a_at(xb, q):
        return a_buf.at[pl.ds(pl.multiple_of(xb * TPD, TPD), TPD), pl.ds(pl.multiple_of(q * FEAT, FEAT), FEAT)]

    def b_at(xw, yw, zw, n=1):
        return b_buf.at[pl.ds(pl.multiple_of(((xw * 4 + yw) * 4 + zw) * ROWS, ROWS), n * ROWS), :]

    def got(ref, rid):
        remote(ref, ref, 0, rid, dev(c_=1 - c)).wait_recv()

    def sent(ref, sid):
        remote(ref, ref, sid, 0, dev(c_=1 - c)).wait_send()

    for e in range(2):
        for p, w in enumerate((wq, wk, wv)):
            for j in range(3):
                cols = slice(e * NC + j * 128, e * NC + (j + 1) * 128)
                ws[e, :, p * NC + j * 128 : p * NC + (j + 1) * 128] = (w[:, cols].astype(jnp.float32) * gn[...]).astype(jnp.bfloat16)
    mbuf[x] = mk[...]

    barrier = pltpu.get_barrier_semaphore()
    for dx in range(4):
        for dc in range(2):
            if dx or dc:
                pl.semaphore_signal(barrier, inc=1, device_id=dev(x_=(x + dx) % 4, c_=(c + dc) % 2), device_id_type=MESH)
    for core in range(2):
        pl.semaphore_signal(barrier, inc=1, device_id=dev(zlo_=1 - zlo, c_=core), device_id_type=MESH)
    for other in (dev(y_=yp), dev(y_=ym), dev(zh_=zp), dev(zh_=zm)):
        pl.semaphore_signal(barrier, inc=1, device_id=other, device_id_type=MESH)
    pl.semaphore_wait(barrier, 13)

    def swap(e):
        here = b_at(x, y, zh)
        away = jnp.logical_or(c + 2 * e != x, x // 2 != c)
        return away, remote(ws.at[e], here, SW + e, SW + x % 2, dev(x_=c + 2 * e, c_=x // 2)), pltpu.make_async_copy(
            ws.at[e], here, rsem.at[SW + x % 2]
        )

    for e in range(2):
        away, far, near = swap(e)

        @pl.when(away)
        def _():
            far.start()

        @pl.when(jnp.logical_not(away))
        def _():
            near.start()

    def first(r, dst_dev, base):
        return remote(tok.at[pl.ds(r * TPD, TPD), :], a_at(x, t), base + r, base + c, dst_dev)

    for r in range(2):
        first(r, dev(x_=xp, c_=r), AXP).start()
        first(r, dev(x_=xm, c_=r), AXM).start()
    across = remote(tok.at[pl.ds(pl.multiple_of((1 - c) * TPD, TPD), TPD), :], a_at(x, t), AD, AD, dev(c_=1 - c))
    across.start()
    own = pltpu.make_async_copy(tok.at[pl.ds(pl.multiple_of(c * TPD, TPD), TPD), :], a_at(x, t), rsem.at[AL])
    own.start()
    for k in range(3):
        remote(mk, mbuf.at[x], MK + k, MK + k, dev(x_=(x + k + 1) % 4)).start()

    xw = [2 * c, 2 * c + 1]

    def y_out(k, z):
        for h in range(2):
            piece = b_at(xw[h], y, z)
            remote(piece, piece, YP + 2 * k + h, YP + 2 * k + h, dev(y_=yp)).start()
            remote(piece, piece, YM + 2 * k + h, YM + 2 * k + h, dev(y_=ym)).start()
            remote(piece, piece, DO + 2 * k + h, DO + 2 * k + h, dev(c_=1 - c)).start()

    for h in range(2):
        piece = b_at(xw[h], y, zh)
        got(piece, SW + h)
        remote(piece, piece, ZP + h, ZP + h, dev(zh_=zp)).start()
        remote(piece, piece, ZM + h, ZM + h, dev(zh_=zm)).start()
    y_out(0, zh)

    acc[...] = jnp.zeros_like(acc)
    s1[...] = jnp.zeros_like(s1)
    s2[...] = jnp.zeros_like(s2)

    for h in range(2):
        got(b_at(xw[h], y, zm), ZP + h)
    piece = b_at(xw[0], y, zm)
    remote(piece, piece, ZFP, ZFP, dev(zh_=zp)).start()
    for h in range(2):
        got(b_at(xw[h], y, zp), ZM + h)
    piece = b_at(xw[1], y, zp)
    remote(piece, piece, ZFM, ZFM, dev(zh_=zm)).start()
    for r in range(2):
        first(r, dev(zlo_=1 - zlo, c_=r), AZ).start()
    y_out(1, zm)
    y_out(2, zp)
    got(b_at(xw[0], y, zo), ZFP)
    got(b_at(xw[1], y, zo), ZFM)
    y_out(3, zo)

    zs = [zh, zp, zm, zo]

    def y_step(k):
        z = [zh, zm, zp, zo][k]
        for h in range(2):
            got(b_at(xw[h], ym, z), YP + 2 * k + h)
        piece = b_at(xw[0], ym, z)
        remote(piece, piece, YFP + k, YFP + k, dev(y_=yp)).start()
        for h in range(2):
            got(b_at(xw[h], yp, z), YM + 2 * k + h)
        piece = b_at(xw[1], yp, z)
        remote(piece, piece, YFM + k, YFM + k, dev(y_=ym)).start()

    y_step(0)
    y_step(1)
    for q in range(2):
        got(a_at(xm, 2 * zlo + q), AXP + q)
        got(a_at(xp, 2 * zlo + q), AXM + q)
    piece = a_at(xm, 2 * zlo)
    remote(piece, piece, AOP, AOP, dev(x_=xp)).start()
    piece = a_at(xp, 2 * zlo + 1)
    remote(piece, piece, AOM, AOM, dev(x_=xm)).start()
    y_step(2)
    for q in range(2):
        piece = a_at(x, 2 * (1 - zlo) + q)
        got(piece, AZ + q)
        remote(piece, piece, AIIP + q, AIIP + q, dev(x_=xp)).start()
        remote(piece, piece, AIIM + q, AIIM + q, dev(x_=xm)).start()
    y_step(3)
    for base, yy in ((DYM, ym), (DYP, yp)):
        for h in range(2):
            chunk = b_at(xw[h], yy, 0, 4)
            remote(chunk, chunk, base + h, base + h, dev(c_=1 - c)).start()
    for q, num in enumerate((AOP, AOM)):
        piece = a_at(xo, 2 * zlo + q)
        got(piece, num)
        remote(piece, piece, AIII + q, AIII + q, dev(zlo_=1 - zlo)).start()
    for h, num in enumerate((YFP, YFM)):
        for k in range(4):
            got(b_at(xw[h], yo, [zh, zm, zp, zo][k]), num + k)
        chunk = b_at(xw[h], yo, 0, 4)
        remote(chunk, chunk, DYO + h, DYO + h, dev(c_=1 - c)).start()
    xv = [2 * (1 - c), 2 * (1 - c) + 1]
    for h in range(2):
        for k in range(4):
            got(b_at(xv[h], y, [zh, zm, zp, zo][k]), DO + 2 * k + h)
    for base, yy in ((DYM, ym), (DYP, yp), (DYO, yo)):
        for h in range(2):
            got(b_at(xv[h], yy, 0, 4), base + h)
    got(a_at(x, 2 * zlo + 1 - c), AD)
    own.wait()
    for k in range(3):
        got(mbuf.at[(x + 3 - k) % 4], MK + k)

    def add_cols(i, total):
        rows = b_buf[pl.ds(pl.multiple_of(i * 32, 32), 32), :].astype(jnp.float32)
        return total + (rows[:8] + rows[8:16]) + (rows[16:24] + rows[24:])

    total = lax.fori_loop(0, D // 32, add_cols, jnp.zeros((8, N), jnp.float32))
    cs[...] = jnp.broadcast_to(jnp.sum(total, axis=0, keepdims=True), (8, N))

    def unit(xb, q):
        row = pl.multiple_of(xb * TPD, TPD)
        col = pl.multiple_of(q * FEAT, FEAT)
        acc[pl.ds(row, TPD), :] += jnp.dot(
            a_buf[pl.ds(row, TPD), pl.ds(col, FEAT)], b_buf[pl.ds(col, FEAT), :], preferred_element_type=jnp.float32
        )

        def stat(i, _):
            rr = pl.multiple_of(row + i * 64, 64)
            t1 = s1[pl.ds(rr, 64), :]
            t2 = s2[pl.ds(rr, 64), :]
            for j in range(FEAT // 128):
                v = a_buf[pl.ds(rr, 64), pl.ds(pl.multiple_of(col + j * 128, 128), 128)].astype(jnp.float32)
                t1 = t1 + v
                t2 = t2 + v * v
            s1[pl.ds(rr, 64), :] = t1
            s2[pl.ds(rr, 64), :] = t2
            return 0

        lax.fori_loop(0, TPD // 64, stat, 0)

    def order(i):
        return (x + jnp.where(i == 1, 3, jnp.where(i == 2, 1, jnp.where(i == 3, 2, 0)))) % 4

    def near(i, _):
        unit(order(i // 2), 2 * zlo + i % 2)
        return 0

    lax.fori_loop(0, 8, near, 0)

    def out_copy(xb, i):
        src = obuf.at[i]
        dst = out.at[pl.ds(pl.multiple_of(c * TPD, TPD), TPD), pl.ds(pl.multiple_of((x // 2) * NC, NC), NC)]
        rid = OUT + 2 * (x // 2) + c
        away = jnp.logical_or(xb != x, x % 2 != c)
        return away, remote(src, dst, OUT + i, rid, dev(x_=xb, c_=x % 2)), pltpu.make_async_copy(src, dst, rsem.at[rid])

    def finish(i, _):
        xb = order(i)
        for k, (num, blk) in enumerate(((AIIP, xm), (AIIM, xp), (AIII, xo))):

            @pl.when(i == k + 1)
            def _():
                for q in range(2):
                    got(a_at(blk, 2 * (1 - zlo) + q), num + q)

        def rest(q, _):
            unit(xb, 2 * (1 - zlo) + q)
            return 0

        lax.fori_loop(0, 2, rest, 0)
        row = pl.multiple_of(xb * TPD, TPD)
        mean = jnp.sum(s1[pl.ds(row, TPD), :], axis=-1, keepdims=True) * (1.0 / D)
        mean_sq = jnp.sum(s2[pl.ds(row, TPD), :], axis=-1, keepdims=True) * (1.0 / D)
        rstd = lax.rsqrt(mean_sq - mean * mean + EPS)

        def part(p, j):
            cols = slice(p * NC + j * DH, p * NC + (j + 1) * DH)
            return (acc[pl.ds(row, TPD), cols] - mean * cs[0:1, cols]) * rstd

        def head_norm(values, gain):
            ms = jnp.mean(values * values, axis=-1, keepdims=True)
            return (values * lax.rsqrt(ms + EPS) * gain).astype(jnp.bfloat16)

        allowed = mbuf[xb]
        seen = jnp.concatenate(
            [jnp.broadcast_to(jnp.where(c == 0, allowed[b : b + 1], allowed[8 + b : 9 + b]), (BLOCK, TPD)) for b in range(4)], axis=0
        )
        for j in range(3):
            qn = head_norm(part(0, j), qg[...])
            kn = head_norm(part(1, j), kg[...])
            v = part(2, j).astype(jnp.bfloat16)
            s = lax.dot_general(qn, kn, (((1,), (1,)), ((), ())), preferred_element_type=jnp.float32) * (1.0 / DH**0.5)
            s = jnp.where(seen > 0, s, jnp.float32(-1e30))
            w = jnp.exp(s - jnp.max(s, axis=-1, keepdims=True))
            probs = (w / jnp.sum(w, axis=-1, keepdims=True)).astype(jnp.bfloat16)
            obuf[i, :, j * DH : (j + 1) * DH] = jnp.dot(probs, v, preferred_element_type=jnp.float32).astype(jnp.bfloat16)
        away, far, near_ = out_copy(xb, i)

        @pl.when(away)
        def _():
            far.start()

        @pl.when(jnp.logical_not(away))
        def _():
            near_.start()

        return 0

    lax.fori_loop(0, 4, finish, 0)

    for e in range(2):
        for r in range(2):
            got(out.at[pl.ds(r * TPD, TPD), pl.ds(e * NC, NC)], OUT + 2 * e + r)
    a_piece = a_at(x, t)
    b_piece = b_at(x, y, zh)
    for num in (AXP, AXP + 1, AXM, AXM + 1, AZ, AZ + 1, AD, AOP, AOM, AIIP, AIIP + 1, AIIM, AIIM + 1, AIII, AIII + 1):
        sent(a_piece, num)
    for k in range(3):
        sent(mk, MK + k)
    for e in range(2):
        away, far, _ = swap(e)

        @pl.when(away)
        def _():
            far.wait_send()

    for num in range(ZP, DYM):
        sent(b_piece, num)
    for num in range(DYM, OUT):
        sent(b_at(x, y, 0, 4), num)
    for i in range(4):
        away, far, _ = out_copy(order(i), i)

        @pl.when(away)
        def _():
            far.wait_send()


def per_device(tokens, block_mask, norm_gain, w_query, w_key, w_value, query_gain, key_gain):
    blocks = block_mask.shape[-1]
    allowed = (block_mask > 0) | (jnp.arange(blocks)[:, None] == jnp.arange(blocks)[None, :])[None]
    allowed = jnp.repeat(allowed.astype(jnp.float32), BLOCK, axis=2)
    allowed = jnp.pad(allowed, ((0, 0), (0, 8 - blocks), (0, 0))).reshape(16, TPD)
    gain = lax.dynamic_slice(norm_gain, (lax.axis_index("dp") * ROWS,), (ROWS,))
    gain = jnp.broadcast_to(gain[:, None], (ROWS, 128))
    vmem = pl.BlockSpec(memory_space=pltpu.VMEM)
    return pl.pallas_call(
        kernel,
        out_shape=jax.ShapeDtypeStruct((512, 768), jnp.bfloat16),
        in_specs=[pl.BlockSpec(memory_space=pl.ANY)] + [vmem] * 7,
        out_specs=pl.BlockSpec(memory_space=pl.ANY),
        scratch_shapes=[
            pltpu.VMEM((4 * TPD, D), jnp.bfloat16),
            pltpu.VMEM((D, N), jnp.bfloat16),
            pltpu.VMEM((2, ROWS, N), jnp.bfloat16),
            pltpu.VMEM((4 * TPD, N), jnp.float32),
            pltpu.VMEM((4 * TPD, 128), jnp.float32),
            pltpu.VMEM((4 * TPD, 128), jnp.float32),
            pltpu.VMEM((8, N), jnp.float32),
            pltpu.VMEM((4, 16, TPD), jnp.float32),
            pltpu.VMEM((4, TPD, NC), jnp.bfloat16),
            pltpu.SemaphoreType.DMA((COUNT,)),
            pltpu.SemaphoreType.DMA((COUNT,)),
        ],
        compiler_params=pltpu.CompilerParams(collective_id=0, has_side_effects=True, vmem_limit_bytes=60 << 20),
    )(tokens, allowed, gain, w_query, w_key, w_value, query_gain.reshape(1, DH), key_gain.reshape(1, DH))


def solution(mesh):
    return jax.shard_map(
        per_device,
        mesh=mesh,
        in_specs=(
            P("dp", "tensor"),
            P("dp", None, None),
            P(),
            P("dp", "tensor"),
            P("dp", "tensor"),
            P("dp", "tensor"),
            P(),
            P(),
        ),
        out_specs=P("dp", "tensor"),
        check_vma=False,
    )
```

```python
import jax
import jax.numpy as jnp
from jax import lax
from jax.experimental import pallas as pl
from jax.experimental.pallas import tpu as pltpu
from jax.sharding import PartitionSpec as P

DH = 128
TPD = 256
BLOCK = 64
EPS = 1e-06
MESH = pl.DeviceIdType.MESH

ROWS = 96
FEAT = 1536
D = 6144
NC = 384
N = 3 * NC

AXP, AXM, AZ, AZL = 0, 2, 4, 6
AD, AL, AOP, AOM = 8, 9, 10, 11
AIIP, AIIM, AIII = 12, 14, 16
AFP, AFM = 18, 19
MK = 20
ST = 23
SW = 26
ZP, ZM, ZFP, ZFM = 28, 30, 32, 33
YP, YM = 34, 42
YFP, YFM = 50, 54
DO = 58
DYM, DYP, DYO = 66, 68, 70
OUT = 72
TOK = 76
COUNT = 77
AHEAD = 64
BYX = 64


def kernel(
    tok, bm, gn, wq, wk, wv, qg, kg, out, tv, nv, st, sg, a_buf, b_buf, acc, mk, mbuf, obuf, ssem, rsem
):
    dp = lax.axis_index("dp")
    t = lax.axis_index("tensor")
    x, y, zh = dp // 16, (dp // 4) % 4, dp % 4
    zlo, c = t // 2, t % 2
    xp, xm, xo = (x + 1) % 4, (x + 3) % 4, (x + 2) % 4
    yp, ym, yo = (y + 1) % 4, (y + 3) % 4, (y + 2) % 4
    zp, zm, zo = (zh + 1) % 4, (zh + 3) % 4, (zh + 2) % 4

    def dev(x_=None, y_=None, zh_=None, zlo_=None, c_=None):
        x_ = x if x_ is None else x_
        y_ = y if y_ is None else y_
        zh_ = zh if zh_ is None else zh_
        zlo_ = zlo if zlo_ is None else zlo_
        c_ = c if c_ is None else c_
        return (x_ * 16 + y_ * 4 + zh_, zlo_ * 2 + c_)

    def remote(src, dst, sid, rid, device):
        return pltpu.make_async_remote_copy(
            src_ref=src, dst_ref=dst, send_sem=ssem.at[sid], recv_sem=rsem.at[rid], device_id=device, device_id_type=MESH
        )

    def a_at(xb, q, r0=0, rows=TPD):
        return a_buf.at[pl.ds(pl.multiple_of(xb * TPD + r0, 64), rows), pl.ds(pl.multiple_of(q * FEAT, FEAT), FEAT)]

    def b_at(xw, yw, zw, n=1):
        return b_buf.at[pl.ds(pl.multiple_of(((xw * 4 + yw) * 4 + zw) * ROWS, ROWS), n * ROWS), :]

    def got(ref, rid):
        remote(ref, ref, 0, rid, dev(c_=1 - c)).wait_recv()

    def sent(ref, sid):
        remote(ref, ref, sid, 0, dev(c_=1 - c)).wait_send()

    def relay(ref, num, device):
        remote(ref, ref, num, num, device).start()

    load = pltpu.make_async_copy(tok, tv, rsem.at[TOK])
    load.start()

    barrier = pltpu.get_barrier_semaphore()
    for dx in range(4):
        for dc in range(2):
            if dx or dc:
                pl.semaphore_signal(barrier, inc=1, device_id=dev(x_=(x + dx) % 4, c_=(c + dc) % 2), device_id_type=MESH)
    for core in range(2):
        pl.semaphore_signal(barrier, inc=1, device_id=dev(zlo_=1 - zlo, c_=core), device_id_type=MESH)
    for other in (dev(y_=yp), dev(y_=ym), dev(zh_=zp), dev(zh_=zm)):
        pl.semaphore_signal(barrier, inc=1, device_id=other, device_id_type=MESH)

    kb = lax.broadcasted_iota(jnp.int32, (4, TPD), 1) // BLOCK
    qb = lax.broadcasted_iota(jnp.int32, (4, TPD), 0)
    for r in range(2):
        m = bm[r]
        seen = jnp.where(kb == 0, m[:, 0:1], jnp.where(kb == 1, m[:, 1:2], jnp.where(kb == 2, m[:, 2:3], m[:, 3:4])))
        mk[8 * r : 8 * r + 4, :] = jnp.where(jnp.logical_or(seen > 0, kb == qb), 1.0, 0.0)
        mk[8 * r + 4 : 8 * r + 8, :] = jnp.zeros((4, TPD), jnp.float32)
    mbuf[x] = mk[...]

    load.wait()
    lane = lax.broadcasted_iota(jnp.int32, (64, 128), 1)

    def stats(i, _):
        rr = pl.multiple_of(i * 64, 64)
        t1 = jnp.zeros((64, 128), jnp.float32)
        t2 = jnp.zeros((64, 128), jnp.float32)
        for j in range(FEAT // 128):
            v = tv[pl.ds(rr, 64), j * 128 : (j + 1) * 128].astype(jnp.float32)
            t1 = t1 + v
            t2 = t2 + v * v
        a1 = jnp.sum(t1, axis=-1, keepdims=True)
        a2 = jnp.sum(t2, axis=-1, keepdims=True)
        st[pl.ds(rr, 64), :] = jnp.where(lane == 0, a1, jnp.where(lane == 1, a2, 0.0))
        return 0

    lax.fori_loop(0, 8, stats, 0)
    for i in range(4):
        sg[t, :, i * 128 : (i + 1) * 128] = jnp.transpose(st[i * 128 : (i + 1) * 128, :])[:8]

    pl.semaphore_wait(barrier, 13)

    def swap(e, p, w):
        src = w.at[:, pl.ds(e * NC, NC)]
        here = b_at(x, y, zh).at[:, pl.ds(p * NC, NC)]
        away = jnp.logical_or(c + 2 * e != x, x // 2 != c)
        far = remote(src, here, SW + e, SW + x % 2, dev(x_=c + 2 * e, c_=x // 2))
        return away, far, pltpu.make_async_copy(src, here, rsem.at[SW + x % 2])

    for e in range(2):
        for p, w in enumerate((wq, wk, wv)):
            away, far, near = swap(e, p, w)

            @pl.when(away)
            def _():
                far.start()

            @pl.when(jnp.logical_not(away))
            def _():
                near.start()

    peers = [dev(c_=1 - c), dev(zlo_=1 - zlo), dev(zlo_=1 - zlo, c_=1 - c)]
    for k in range(3):
        remote(sg.at[t], sg.at[t], ST + k, ST + k, peers[k]).start()
    for k in range(3):
        remote(mk, mbuf.at[x], MK + k, MK + k, dev(x_=(x + k + 1) % 4)).start()
    theirs = [t + 1 - 2 * c, (t + 2) % 4, (t + 2) % 4 + 1 - 2 * c]
    for k in range(3):
        got(sg.at[theirs[k]], ST + k)
    total = (sg[0] + sg[1]) + (sg[2] + sg[3])
    mean = total[0:1] * (1.0 / D)
    rstd = lax.rsqrt(total[1:2] * (1.0 / D) - mean * mean + EPS)
    row = lax.broadcasted_iota(jnp.int32, (128, 128), 0)
    for i in range(4):
        cols = slice(i * 128, (i + 1) * 128)
        st[i * 128 : (i + 1) * 128, :] = jnp.transpose(jnp.where(row == 0, mean[:, cols], rstd[:, cols]))

    def norm(i, _):
        rr = pl.multiple_of(i * 64, 64)
        mu = jnp.broadcast_to(st[pl.ds(rr, 64), 0:1], (64, 128))
        rs = jnp.broadcast_to(st[pl.ds(rr, 64), 1:2], (64, 128))
        for j in range(FEAT // 128):
            v = tv[pl.ds(rr, 64), j * 128 : (j + 1) * 128].astype(jnp.float32)
            g = gn[:, pl.ds(pl.multiple_of(t * FEAT + j * 128, 128), 128)]
            nv[pl.ds(rr, 64), j * 128 : (j + 1) * 128] = ((v - mu) * rs * g).astype(jnp.bfloat16)
        return 0

    lax.fori_loop(0, 8, norm, 0)

    def first(r, dst_dev, base, r0=0, rows=TPD):
        return remote(nv.at[pl.ds(r * TPD + r0, rows), :], a_at(x, t, r0, rows), base + r, base + c, dst_dev)

    def pair(r, r0, rows, base):
        return first(r, dev(zlo_=1 - zlo, c_=r), base, r0, rows)

    for r in range(2):
        first(r, dev(x_=xp, c_=r), AXP).start()
        first(r, dev(x_=xm, c_=r), AXM).start()
        pair(r, 0, AHEAD, AZ).start()
    half = nv.at[pl.ds(pl.multiple_of((1 - c) * TPD, TPD), TPD), :]
    remote(half, a_at(x, t), AD, AD, dev(c_=1 - c)).start()
    own = pltpu.make_async_copy(nv.at[pl.ds(pl.multiple_of(c * TPD, TPD), TPD), :], a_at(x, t), rsem.at[AL])
    own.start()

    xw = [2 * c, 2 * c + 1]
    names = [zh, zm, zp, zo]

    def y_out(k, h):
        piece = b_at(xw[h], y, names[k])
        relay(piece, YP + 2 * k + h, dev(y_=yp))
        relay(piece, YM + 2 * k + h, dev(y_=ym))
        relay(piece, DO + 2 * k + h, dev(c_=1 - c))

    def y_on(k, h):
        got(b_at(xw[h], ym, names[k]), YP + 2 * k + h)
        if h == 0:
            relay(b_at(xw[0], ym, names[k]), YFP + k, dev(y_=yp))
        got(b_at(xw[h], yp, names[k]), YM + 2 * k + h)
        if h == 1:
            relay(b_at(xw[1], yp, names[k]), YFM + k, dev(y_=ym))

    for h in range(2):
        piece = b_at(xw[h], y, zh)
        got(piece, SW + h)
        relay(piece, ZP + h, dev(zh_=zp))
        relay(piece, ZM + h, dev(zh_=zm))
        y_out(0, h)

    acc[...] = jnp.zeros_like(acc)
    y_on(0, 0)
    got(b_at(xw[0], y, zm), ZP)
    relay(b_at(xw[0], y, zm), ZFP, dev(zh_=zp))
    y_out(1, 0)
    got(b_at(xw[0], y, zp), ZM)
    y_out(2, 0)
    y_on(0, 1)
    got(b_at(xw[1], y, zm), ZP + 1)
    y_out(1, 1)
    got(b_at(xw[1], y, zp), ZM + 1)
    relay(b_at(xw[1], y, zp), ZFM, dev(zh_=zm))
    y_out(2, 1)
    for r in range(2):
        pair(r, AHEAD, TPD - AHEAD, AZL).start()
    y_on(1, 0)
    y_on(2, 0)
    got(b_at(xw[0], y, zo), ZFP)
    y_out(3, 0)
    got(b_at(xw[1], y, zo), ZFM)
    y_out(3, 1)
    y_on(1, 1)
    for q in range(2):
        got(a_at(xm, 2 * zlo + q), AXP + q)
        got(a_at(xp, 2 * zlo + q), AXM + q)
        if q == 0:
            relay(a_at(xm, 2 * zlo), AOP, dev(x_=xp))
    relay(a_at(xp, 2 * zlo + 1), AOM, dev(x_=xm))
    y_on(2, 1)
    y_on(3, 0)
    y_on(3, 1)
    for base, yy in ((DYM, ym), (DYP, yp)):
        for h in range(2):
            relay(b_at(xw[h], yy, 0, 4), base + h, dev(c_=1 - c))
    for q in range(2):
        got(a_at(x, 2 * (1 - zlo) + q, 0, AHEAD), AZ + q)
        got(a_at(x, 2 * (1 - zlo) + q, AHEAD, TPD - AHEAD), AZL + q)
        piece = a_at(x, 2 * (1 - zlo) + q)
        relay(piece, AIIP + q, dev(x_=xp))
        relay(piece, AIIM + q, dev(x_=xm))
    got(a_at(xo, 2 * zlo), AOP)
    relay(a_at(xo, 2 * zlo), AIII, dev(zlo_=1 - zlo))
    got(a_at(xo, 2 * zlo + 1), AOM)
    relay(a_at(xo, 2 * zlo + 1, 0, TPD - 2 * BYX), AIII + 1, dev(zlo_=1 - zlo))
    for k in range(4):
        got(b_at(xw[0], yo, names[k]), YFP + k)
        got(b_at(xw[1], yo, names[k]), YFM + k)
    for h in range(2):
        relay(b_at(xw[h], yo, 0, 4), DYO + h, dev(c_=1 - c))
    xv = [2 * (1 - c), 2 * (1 - c) + 1]
    for h in range(2):
        for k in range(4):
            got(b_at(xv[h], y, names[k]), DO + 2 * k + h)
    for base, yy in ((DYM, ym), (DYP, yp), (DYO, yo)):
        for h in range(2):
            got(b_at(xv[h], yy, 0, 4), base + h)
    got(a_at(x, 2 * zlo + 1 - c), AD)
    own.wait()
    for k in range(3):
        got(mbuf.at[(x + 3 - k) % 4], MK + k)

    def unit(xb, q):
        row = pl.multiple_of(xb * TPD, TPD)
        col = pl.multiple_of(q * FEAT, FEAT)
        acc[pl.ds(row, TPD), :] += jnp.dot(
            a_buf[pl.ds(row, TPD), pl.ds(col, FEAT)], b_buf[pl.ds(col, FEAT), :], preferred_element_type=jnp.float32
        )

    def order(i):
        return (x + jnp.where(i == 1, 3, jnp.where(i == 2, 1, jnp.where(i == 3, 2, 0)))) % 4

    def near(i, _):
        b = jnp.where(i < 4, 0, i // 2 - 1)
        q = jnp.where(i < 4, i % 4, i % 2)
        unit(order(b), (2 * zlo + q) % 4)
        return 0

    lax.fori_loop(0, 10, near, 0)

    def out_copy(xb, i):
        src = obuf.at[i]
        dst = out.at[pl.ds(pl.multiple_of(c * TPD, TPD), TPD), pl.ds(pl.multiple_of((x // 2) * NC, NC), NC)]
        rid = OUT + 2 * (x // 2) + c
        away = jnp.logical_or(xb != x, x % 2 != c)
        return away, remote(src, dst, OUT + i, rid, dev(x_=xb, c_=x % 2)), pltpu.make_async_copy(src, dst, rsem.at[rid])

    def finish(i):
        xb = order(i)
        row = pl.multiple_of(xb * TPD, TPD)

        def part(p, j):
            return acc[pl.ds(row, TPD), p * NC + j * DH : p * NC + (j + 1) * DH]

        def head_norm(values, gain):
            ms = jnp.mean(values * values, axis=-1, keepdims=True)
            return (values * lax.rsqrt(ms + EPS) * gain).astype(jnp.bfloat16)

        allowed = mbuf[xb]
        seen = jnp.concatenate(
            [jnp.broadcast_to(jnp.where(c == 0, allowed[b : b + 1], allowed[8 + b : 9 + b]), (BLOCK, TPD)) for b in range(4)], axis=0
        )
        for j in range(3):
            qn = head_norm(part(0, j), qg[...])
            kn = head_norm(part(1, j), kg[...])
            v = part(2, j).astype(jnp.bfloat16)
            s = lax.dot_general(qn, kn, (((1,), (1,)), ((), ())), preferred_element_type=jnp.float32) * (1.0 / DH**0.5)
            s = jnp.where(seen > 0, s, jnp.float32(-1e30))
            w = jnp.exp(s - jnp.max(s, axis=-1, keepdims=True))
            probs = (w / jnp.sum(w, axis=-1, keepdims=True)).astype(jnp.bfloat16)
            obuf[i, :, j * DH : (j + 1) * DH] = jnp.dot(probs, v, preferred_element_type=jnp.float32).astype(jnp.bfloat16)
        away, far, near_ = out_copy(xb, i)

        @pl.when(away)
        def _():
            far.start()

        @pl.when(jnp.logical_not(away))
        def _():
            near_.start()

    finish(0)

    def third(i, _):
        for k, (num, blk) in enumerate(((AIIP, xm), (AIIM, xp), (AIII, xo))):

            @pl.when(i == k + 1)
            def _():
                got(a_at(blk, 2 * (1 - zlo)), num)

        unit(order(i), 2 * (1 - zlo))
        return 0

    lax.fori_loop(1, 4, third, 0)
    far_q = 2 * (1 - zlo) + 1
    got(a_at(xm, far_q), AIIP + 1)
    relay(a_at(xm, far_q, TPD - 2 * BYX, BYX), AFP, dev(x_=xp))
    got(a_at(xp, far_q), AIIM + 1)
    relay(a_at(xp, far_q, TPD - BYX, BYX), AFM, dev(x_=xm))

    def last(i, _):
        @pl.when(i == 3)
        def _():
            got(a_at(xo, far_q, 0, TPD - 2 * BYX), AIII + 1)
            got(a_at(xo, far_q, TPD - 2 * BYX, BYX), AFP)
            got(a_at(xo, far_q, TPD - BYX, BYX), AFM)

        unit(order(i), far_q)
        finish(i)
        return 0

    lax.fori_loop(1, 4, last, 0)

    for e in range(2):
        for r in range(2):
            got(out.at[pl.ds(r * TPD, TPD), pl.ds(e * NC, NC)], OUT + 2 * e + r)
    for num in (AXP, AXP + 1, AXM, AXM + 1, AD, AOP, AOM, AIIP, AIIP + 1, AIIM, AIIM + 1, AIII):
        sent(a_at(x, t), num)
    sent(a_at(x, t, 0, TPD - 2 * BYX), AIII + 1)
    for r in range(2):
        sent(a_at(x, t, 0, AHEAD), AZ + r)
        sent(a_at(x, t, AHEAD, TPD - AHEAD), AZL + r)
    for num in (AFP, AFM):
        sent(a_at(x, t, 0, BYX), num)
    for k in range(3):
        sent(mk, MK + k)
        sent(sg.at[t], ST + k)
    for e in range(2):

        @pl.when(jnp.logical_or(c + 2 * e != x, x // 2 != c))
        def _():
            sent(b_at(x, y, zh), SW + e)

    for num in range(ZP, DYM):
        sent(b_at(x, y, zh), num)
    for num in range(DYM, OUT):
        sent(b_at(x, y, 0, 4), num)
    for i in range(4):
        away, far, _ = out_copy(order(i), i)

        @pl.when(away)
        def _():
            far.wait_send()


def per_device(tokens, block_mask, norm_gain, w_query, w_key, w_value, query_gain, key_gain):
    vmem = pl.BlockSpec(memory_space=pltpu.VMEM)
    hbm = pl.BlockSpec(memory_space=pl.ANY)
    return pl.pallas_call(
        kernel,
        out_shape=jax.ShapeDtypeStruct((512, 768), jnp.bfloat16),
        in_specs=[hbm, vmem, vmem, hbm, hbm, hbm, vmem, vmem],
        out_specs=hbm,
        scratch_shapes=[
            pltpu.VMEM((2 * TPD, FEAT), jnp.bfloat16),
            pltpu.VMEM((2 * TPD, FEAT), jnp.bfloat16),
            pltpu.VMEM((2 * TPD, 128), jnp.float32),
            pltpu.VMEM((4, 8, 2 * TPD), jnp.float32),
            pltpu.VMEM((4 * TPD, D), jnp.bfloat16),
            pltpu.VMEM((D, N), jnp.bfloat16),
            pltpu.VMEM((4 * TPD, N), jnp.float32),
            pltpu.VMEM((16, TPD), jnp.float32),
            pltpu.VMEM((4, 16, TPD), jnp.float32),
            pltpu.VMEM((4, TPD, NC), jnp.bfloat16),
            pltpu.SemaphoreType.DMA((COUNT,)),
            pltpu.SemaphoreType.DMA((COUNT,)),
        ],
        compiler_params=pltpu.CompilerParams(collective_id=0, has_side_effects=True, vmem_limit_bytes=60 << 20),
    )(tokens, block_mask, norm_gain.reshape(1, D), w_query, w_key, w_value, query_gain.reshape(1, DH), key_gain.reshape(1, DH))


def solution(mesh):
    return jax.shard_map(
        per_device,
        mesh=mesh,
        in_specs=(
            P("dp", "tensor"),
            P("dp", None, None),
            P(),
            P("dp", "tensor"),
            P("dp", "tensor"),
            P("dp", "tensor"),
            P(),
            P(),
        ),
        out_specs=P("dp", "tensor"),
        check_vma=False,
    )
```

```python
import jax
import jax.numpy as jnp
from jax import lax
from jax.experimental import pallas as pl
from jax.experimental.pallas import tpu as pltpu
from jax.sharding import PartitionSpec as P

DH = 128
TPD = 256
BLOCK = 64
EPS = 1e-06
MESH = pl.DeviceIdType.MESH

ROWS = 96
FEAT = 1536
D = 6144
NC = 384
N = 3 * NC

AXP, AXM, AZ = 0, 2, 4
AD, AL, AOP, AOM = 8, 9, 10, 11
AIIP, AIIM, AIII = 12, 14, 16
AFP, AFM = 18, 19
MK = 20
ST = 23
SW = 26
ZP, ZM, ZFP, ZFM = 28, 30, 32, 33
YP, YM = 34, 42
YFP, YFM = 50, 54
DO = 58
DYM, DYP, DYO = 66, 68, 70
OUT = 72
TOK = 76
COUNT = 77
BYX = 64


def kernel(
    tok, bm, gn, wq, wk, wv, qg, kg, out, tv, nv, st, sg, a_buf, b_buf, acc, mk, mbuf, obuf, ssem, rsem
):
    dp = lax.axis_index("dp")
    t = lax.axis_index("tensor")
    x, y, zh = dp // 16, (dp // 4) % 4, dp % 4
    zlo, c = t // 2, t % 2
    xp, xm, xo = (x + 1) % 4, (x + 3) % 4, (x + 2) % 4
    yp, ym, yo = (y + 1) % 4, (y + 3) % 4, (y + 2) % 4
    zp, zm, zo = (zh + 1) % 4, (zh + 3) % 4, (zh + 2) % 4

    def dev(x_=None, y_=None, zh_=None, zlo_=None, c_=None):
        x_ = x if x_ is None else x_
        y_ = y if y_ is None else y_
        zh_ = zh if zh_ is None else zh_
        zlo_ = zlo if zlo_ is None else zlo_
        c_ = c if c_ is None else c_
        return (x_ * 16 + y_ * 4 + zh_, zlo_ * 2 + c_)

    def remote(src, dst, sid, rid, device):
        return pltpu.make_async_remote_copy(
            src_ref=src, dst_ref=dst, send_sem=ssem.at[sid], recv_sem=rsem.at[rid], device_id=device, device_id_type=MESH
        )

    def a_at(xb, q, r0=0, rows=TPD):
        return a_buf.at[pl.ds(pl.multiple_of(xb * TPD + r0, 64), rows), pl.ds(pl.multiple_of(q * FEAT, FEAT), FEAT)]

    def b_at(xw, yw, zw, n=1):
        return b_buf.at[pl.ds(pl.multiple_of(((xw * 4 + yw) * 4 + zw) * ROWS, ROWS), n * ROWS), :]

    def got(ref, rid):
        remote(ref, ref, 0, rid, dev(c_=1 - c)).wait_recv()

    def sent(ref, sid):
        remote(ref, ref, sid, 0, dev(c_=1 - c)).wait_send()

    def relay(ref, num, device):
        remote(ref, ref, num, num, device).start()

    load = pltpu.make_async_copy(tok, tv, rsem.at[TOK])
    load.start()

    barrier = pltpu.get_barrier_semaphore()
    for dx in range(4):
        for dc in range(2):
            if dx or dc:
                pl.semaphore_signal(barrier, inc=1, device_id=dev(x_=(x + dx) % 4, c_=(c + dc) % 2), device_id_type=MESH)
    for core in range(2):
        pl.semaphore_signal(barrier, inc=1, device_id=dev(zlo_=1 - zlo, c_=core), device_id_type=MESH)
    for other in (dev(y_=yp), dev(y_=ym), dev(zh_=zp), dev(zh_=zm)):
        pl.semaphore_signal(barrier, inc=1, device_id=other, device_id_type=MESH)

    kb = lax.broadcasted_iota(jnp.int32, (4, TPD), 1) // BLOCK
    qb = lax.broadcasted_iota(jnp.int32, (4, TPD), 0)
    for r in range(2):
        m = bm[r]
        seen = jnp.where(kb == 0, m[:, 0:1], jnp.where(kb == 1, m[:, 1:2], jnp.where(kb == 2, m[:, 2:3], m[:, 3:4])))
        mk[8 * r : 8 * r + 4, :] = jnp.where(jnp.logical_or(seen > 0, kb == qb), 1.0, 0.0)
        mk[8 * r + 4 : 8 * r + 8, :] = jnp.zeros((4, TPD), jnp.float32)
    mbuf[x] = mk[...]

    load.wait()
    lane = lax.broadcasted_iota(jnp.int32, (64, 128), 1)

    def stats(i, _):
        rr = pl.multiple_of(i * 64, 64)
        t1 = jnp.zeros((64, 128), jnp.float32)
        t2 = jnp.zeros((64, 128), jnp.float32)
        for j in range(FEAT // 128):
            v = tv[pl.ds(rr, 64), j * 128 : (j + 1) * 128].astype(jnp.float32)
            t1 = t1 + v
            t2 = t2 + v * v
        a1 = jnp.sum(t1, axis=-1, keepdims=True)
        a2 = jnp.sum(t2, axis=-1, keepdims=True)
        st[pl.ds(rr, 64), :] = jnp.where(lane == 0, a1, jnp.where(lane == 1, a2, 0.0))
        return 0

    lax.fori_loop(0, 8, stats, 0)
    for i in range(4):
        sg[t, :, i * 128 : (i + 1) * 128] = jnp.transpose(st[i * 128 : (i + 1) * 128, :])[:8]

    pl.semaphore_wait(barrier, 13)

    def swap(e, p, w):
        src = w.at[:, pl.ds(e * NC, NC)]
        here = b_at(x, y, zh).at[:, pl.ds(p * NC, NC)]
        away = jnp.logical_or(c + 2 * e != x, x // 2 != c)
        far = remote(src, here, SW + e, SW + x % 2, dev(x_=c + 2 * e, c_=x // 2))
        return away, far, pltpu.make_async_copy(src, here, rsem.at[SW + x % 2])

    for e in range(2):
        for p, w in enumerate((wq, wk, wv)):
            away, far, near = swap(e, p, w)

            @pl.when(away)
            def _():
                far.start()

            @pl.when(jnp.logical_not(away))
            def _():
                near.start()

    peers = [dev(c_=1 - c), dev(zlo_=1 - zlo), dev(zlo_=1 - zlo, c_=1 - c)]
    for k in range(3):
        remote(sg.at[t], sg.at[t], ST + k, ST + k, peers[k]).start()
    for k in range(3):
        remote(mk, mbuf.at[x], MK + k, MK + k, dev(x_=(x + k + 1) % 4)).start()
    theirs = [t + 1 - 2 * c, (t + 2) % 4, (t + 2) % 4 + 1 - 2 * c]
    for k in range(3):
        got(sg.at[theirs[k]], ST + k)
    total = (sg[0] + sg[1]) + (sg[2] + sg[3])
    mean = total[0:1] * (1.0 / D)
    rstd = lax.rsqrt(total[1:2] * (1.0 / D) - mean * mean + EPS)
    row = lax.broadcasted_iota(jnp.int32, (128, 128), 0)
    for i in range(4):
        cols = slice(i * 128, (i + 1) * 128)
        st[i * 128 : (i + 1) * 128, :] = jnp.transpose(jnp.where(row == 0, mean[:, cols], rstd[:, cols]))

    def norm(i, _):
        rr = pl.multiple_of(i * 64, 64)
        mu = jnp.broadcast_to(st[pl.ds(rr, 64), 0:1], (64, 128))
        rs = jnp.broadcast_to(st[pl.ds(rr, 64), 1:2], (64, 128))
        for j in range(FEAT // 128):
            v = tv[pl.ds(rr, 64), j * 128 : (j + 1) * 128].astype(jnp.float32)
            g = gn[:, pl.ds(pl.multiple_of(t * FEAT + j * 128, 128), 128)]
            nv[pl.ds(rr, 64), j * 128 : (j + 1) * 128] = ((v - mu) * rs * g).astype(jnp.bfloat16)
        return 0

    lax.fori_loop(0, 8, norm, 0)

    def first(r, dst_dev, base):
        return remote(nv.at[pl.ds(pl.multiple_of(r * TPD, TPD), TPD), :], a_at(x, t), base + r, base + c, dst_dev)

    turns = [c, 1 - c]
    for r in turns:
        first(r, dev(x_=xp, c_=r), AXP).start()
        first(r, dev(x_=xm, c_=r), AXM).start()
    half = nv.at[pl.ds(pl.multiple_of((1 - c) * TPD, TPD), TPD), :]
    remote(half, a_at(x, t), AD, AD, dev(c_=1 - c)).start()
    own = pltpu.make_async_copy(nv.at[pl.ds(pl.multiple_of(c * TPD, TPD), TPD), :], a_at(x, t), rsem.at[AL])
    own.start()

    xw = [2 * c, 2 * c + 1]
    names = [zh, zm, zp, zo]

    def y_out(k, h):
        piece = b_at(xw[h], y, names[k])
        relay(piece, YP + 2 * k + h, dev(y_=yp))
        relay(piece, YM + 2 * k + h, dev(y_=ym))
        relay(piece, DO + 2 * k + h, dev(c_=1 - c))

    def y_on(k, h):
        got(b_at(xw[h], ym, names[k]), YP + 2 * k + h)
        if h == 0:
            relay(b_at(xw[0], ym, names[k]), YFP + k, dev(y_=yp))
        got(b_at(xw[h], yp, names[k]), YM + 2 * k + h)
        if h == 1:
            relay(b_at(xw[1], yp, names[k]), YFM + k, dev(y_=ym))

    for h in range(2):
        piece = b_at(xw[h], y, zh)
        got(piece, SW + h)
        relay(piece, ZP + h, dev(zh_=zp))
        relay(piece, ZM + h, dev(zh_=zm))
        y_out(0, h)

    acc[...] = jnp.zeros_like(acc)

    def pair_on(q):
        piece = a_at(x, 2 * (1 - zlo) + q)
        got(piece, AZ + q)
        relay(piece, AIIP + q, dev(x_=xp))
        relay(piece, AIIM + q, dev(x_=xm))

    y_on(0, 0)
    got(b_at(xw[0], y, zm), ZP)
    relay(b_at(xw[0], y, zm), ZFP, dev(zh_=zp))
    y_out(1, 0)
    got(b_at(xw[0], y, zp), ZM)
    y_out(2, 0)
    y_on(0, 1)
    got(b_at(xw[1], y, zm), ZP + 1)
    y_out(1, 1)
    got(b_at(xw[1], y, zp), ZM + 1)
    relay(b_at(xw[1], y, zp), ZFM, dev(zh_=zm))
    y_out(2, 1)
    for r in turns:
        first(r, dev(zlo_=1 - zlo, c_=r), AZ).start()
    y_on(1, 0)
    y_on(2, 0)
    got(b_at(xw[0], y, zo), ZFP)
    y_out(3, 0)
    got(b_at(xw[1], y, zo), ZFM)
    y_out(3, 1)
    y_on(1, 1)
    got(a_at(xm, 2 * zlo), AXP)
    relay(a_at(xm, 2 * zlo), AOP, dev(x_=xp))
    got(a_at(xp, 2 * zlo + 1), AXM + 1)
    relay(a_at(xp, 2 * zlo + 1), AOM, dev(x_=xm))
    y_on(2, 1)
    pair_on(c)
    y_on(3, 0)
    y_on(3, 1)
    for base, yy in ((DYM, ym), (DYP, yp)):
        for h in range(2):
            relay(b_at(xw[h], yy, 0, 4), base + h, dev(c_=1 - c))
    pair_on(1 - c)
    got(a_at(xm, 2 * zlo + 1), AXP + 1)
    got(a_at(xp, 2 * zlo), AXM)
    got(a_at(xo, 2 * zlo), AOP)
    relay(a_at(xo, 2 * zlo), AIII, dev(zlo_=1 - zlo))
    got(a_at(xo, 2 * zlo + 1), AOM)
    relay(a_at(xo, 2 * zlo + 1, 0, TPD - 2 * BYX), AIII + 1, dev(zlo_=1 - zlo))
    for k in range(4):
        got(b_at(xw[0], yo, names[k]), YFP + k)
        got(b_at(xw[1], yo, names[k]), YFM + k)
    for h in range(2):
        relay(b_at(xw[h], yo, 0, 4), DYO + h, dev(c_=1 - c))
    xv = [2 * (1 - c), 2 * (1 - c) + 1]
    for h in range(2):
        for k in range(4):
            got(b_at(xv[h], y, names[k]), DO + 2 * k + h)
    for base, yy in ((DYM, ym), (DYP, yp), (DYO, yo)):
        for h in range(2):
            got(b_at(xv[h], yy, 0, 4), base + h)
    got(a_at(x, 2 * zlo + 1 - c), AD)
    own.wait()
    for k in range(3):
        got(mbuf.at[(x + 3 - k) % 4], MK + k)

    def unit(xb, q):
        row = pl.multiple_of(xb * TPD, TPD)
        col = pl.multiple_of(q * FEAT, FEAT)
        acc[pl.ds(row, TPD), :] += jnp.dot(
            a_buf[pl.ds(row, TPD), pl.ds(col, FEAT)], b_buf[pl.ds(col, FEAT), :], preferred_element_type=jnp.float32
        )

    def order(i):
        return (x + jnp.where(i == 1, 3, jnp.where(i == 2, 1, jnp.where(i == 3, 2, 0)))) % 4

    def near(i, _):
        b = jnp.where(i < 4, 0, i // 2 - 1)
        q = jnp.where(i < 4, i % 4, i % 2)
        unit(order(b), (2 * zlo + q) % 4)
        return 0

    lax.fori_loop(0, 10, near, 0)

    def out_copy(xb, i):
        src = obuf.at[i]
        dst = out.at[pl.ds(pl.multiple_of(c * TPD, TPD), TPD), pl.ds(pl.multiple_of((x // 2) * NC, NC), NC)]
        rid = OUT + 2 * (x // 2) + c
        away = jnp.logical_or(xb != x, x % 2 != c)
        return away, remote(src, dst, OUT + i, rid, dev(x_=xb, c_=x % 2)), pltpu.make_async_copy(src, dst, rsem.at[rid])

    def finish(i):
        xb = order(i)
        row = pl.multiple_of(xb * TPD, TPD)

        def part(p, j):
            return acc[pl.ds(row, TPD), p * NC + j * DH : p * NC + (j + 1) * DH]

        def head_norm(values, gain):
            ms = jnp.mean(values * values, axis=-1, keepdims=True)
            return (values * lax.rsqrt(ms + EPS) * gain).astype(jnp.bfloat16)

        allowed = mbuf[xb]
        seen = jnp.concatenate(
            [jnp.broadcast_to(jnp.where(c == 0, allowed[b : b + 1], allowed[8 + b : 9 + b]), (BLOCK, TPD)) for b in range(4)], axis=0
        )
        for j in range(3):
            qn = head_norm(part(0, j), qg[...])
            kn = head_norm(part(1, j), kg[...])
            v = part(2, j).astype(jnp.bfloat16)
            s = lax.dot_general(qn, kn, (((1,), (1,)), ((), ())), preferred_element_type=jnp.float32) * (1.0 / DH**0.5)
            s = jnp.where(seen > 0, s, jnp.float32(-1e30))
            w = jnp.exp(s - jnp.max(s, axis=-1, keepdims=True))
            probs = (w / jnp.sum(w, axis=-1, keepdims=True)).astype(jnp.bfloat16)
            obuf[i, :, j * DH : (j + 1) * DH] = jnp.dot(probs, v, preferred_element_type=jnp.float32).astype(jnp.bfloat16)
        away, far, near_ = out_copy(xb, i)

        @pl.when(away)
        def _():
            far.start()

        @pl.when(jnp.logical_not(away))
        def _():
            near_.start()

    finish(0)

    def third(i, _):
        for k, (num, blk) in enumerate(((AIIP, xm), (AIIM, xp), (AIII, xo))):

            @pl.when(i == k + 1)
            def _():
                got(a_at(blk, 2 * (1 - zlo)), num)

        unit(order(i), 2 * (1 - zlo))
        return 0

    lax.fori_loop(1, 4, third, 0)
    far_q = 2 * (1 - zlo) + 1
    got(a_at(xm, far_q), AIIP + 1)
    relay(a_at(xm, far_q, TPD - 2 * BYX, BYX), AFP, dev(x_=xp))
    got(a_at(xp, far_q), AIIM + 1)
    relay(a_at(xp, far_q, TPD - BYX, BYX), AFM, dev(x_=xm))

    def last(i, _):
        @pl.when(i == 3)
        def _():
            got(a_at(xo, far_q, 0, TPD - 2 * BYX), AIII + 1)
            got(a_at(xo, far_q, TPD - 2 * BYX, BYX), AFP)
            got(a_at(xo, far_q, TPD - BYX, BYX), AFM)

        unit(order(i), far_q)
        finish(i)
        return 0

    lax.fori_loop(1, 4, last, 0)

    for e in range(2):
        for r in range(2):
            got(out.at[pl.ds(r * TPD, TPD), pl.ds(e * NC, NC)], OUT + 2 * e + r)
    for num in (AXP, AXP + 1, AXM, AXM + 1, AD, AOP, AOM, AIIP, AIIP + 1, AIIM, AIIM + 1, AIII):
        sent(a_at(x, t), num)
    sent(a_at(x, t, 0, TPD - 2 * BYX), AIII + 1)
    for r in range(2):
        sent(a_at(x, t), AZ + r)
    for num in (AFP, AFM):
        sent(a_at(x, t, 0, BYX), num)
    for k in range(3):
        sent(mk, MK + k)
        sent(sg.at[t], ST + k)
    for e in range(2):

        @pl.when(jnp.logical_or(c + 2 * e != x, x // 2 != c))
        def _():
            sent(b_at(x, y, zh), SW + e)

    for num in range(ZP, DYM):
        sent(b_at(x, y, zh), num)
    for num in range(DYM, OUT):
        sent(b_at(x, y, 0, 4), num)
    for i in range(4):
        away, far, _ = out_copy(order(i), i)

        @pl.when(away)
        def _():
            far.wait_send()


def per_device(tokens, block_mask, norm_gain, w_query, w_key, w_value, query_gain, key_gain):
    vmem = pl.BlockSpec(memory_space=pltpu.VMEM)
    hbm = pl.BlockSpec(memory_space=pl.ANY)
    return pl.pallas_call(
        kernel,
        out_shape=jax.ShapeDtypeStruct((512, 768), jnp.bfloat16),
        in_specs=[hbm, vmem, vmem, hbm, hbm, hbm, vmem, vmem],
        out_specs=hbm,
        scratch_shapes=[
            pltpu.VMEM((2 * TPD, FEAT), jnp.bfloat16),
            pltpu.VMEM((2 * TPD, FEAT), jnp.bfloat16),
            pltpu.VMEM((2 * TPD, 128), jnp.float32),
            pltpu.VMEM((4, 8, 2 * TPD), jnp.float32),
            pltpu.VMEM((4 * TPD, D), jnp.bfloat16),
            pltpu.VMEM((D, N), jnp.bfloat16),
            pltpu.VMEM((4 * TPD, N), jnp.float32),
            pltpu.VMEM((16, TPD), jnp.float32),
            pltpu.VMEM((4, 16, TPD), jnp.float32),
            pltpu.VMEM((4, TPD, NC), jnp.bfloat16),
            pltpu.SemaphoreType.DMA((COUNT,)),
            pltpu.SemaphoreType.DMA((COUNT,)),
        ],
        compiler_params=pltpu.CompilerParams(collective_id=0, has_side_effects=True, vmem_limit_bytes=60 << 20),
    )(tokens, block_mask, norm_gain.reshape(1, D), w_query, w_key, w_value, query_gain.reshape(1, DH), key_gain.reshape(1, DH))


def solution(mesh):
    return jax.shard_map(
        per_device,
        mesh=mesh,
        in_specs=(
            P("dp", "tensor"),
            P("dp", None, None),
            P(),
            P("dp", "tensor"),
            P("dp", "tensor"),
            P("dp", "tensor"),
            P(),
            P(),
        ),
        out_specs=P("dp", "tensor"),
        check_vma=False,
    )
```

```python
import jax
import jax.numpy as jnp
from jax import lax
from jax.experimental import pallas as pl
from jax.experimental.pallas import tpu as pltpu
from jax.sharding import PartitionSpec as P

DH = 128
TPD = 256
BLOCK = 64
EPS = 1e-06
MESH = pl.DeviceIdType.MESH

ROWS = 96
FEAT = 1536
D = 6144
NC = 384
N = 3 * NC

AXP, AXM, AZ = 0, 2, 4
AD, AL, AOP, AOM = 8, 9, 10, 11
AIIP, AIIM, AIII = 12, 14, 16
AFP, AFM = 18, 19
MK = 20
ST = 23
SW = 26
ZP, ZM, ZFP, ZFM = 28, 30, 32, 33
YP, YM = 34, 42
YFP, YFM = 50, 54
DO = 58
DYM, DYP, DYO = 66, 68, 70
OUT = 72
TOK = 76
ALP, ALM = 77, 78
AQP, AQM, AIV = 79, 80, 81
COUNT = 82
BYX = 96


def kernel(
    tok, bm, gn, wq, wk, wv, qg, kg, out, tv, nv, st, sg, a_buf, b_buf, acc, mk, mbuf, obuf, ssem, rsem
):
    dp = lax.axis_index("dp")
    t = lax.axis_index("tensor")
    x, y, zh = dp // 16, (dp // 4) % 4, dp % 4
    zlo, c = t // 2, t % 2
    xp, xm, xo = (x + 1) % 4, (x + 3) % 4, (x + 2) % 4
    yp, ym, yo = (y + 1) % 4, (y + 3) % 4, (y + 2) % 4
    zp, zm, zo = (zh + 1) % 4, (zh + 3) % 4, (zh + 2) % 4

    def dev(x_=None, y_=None, zh_=None, zlo_=None, c_=None):
        x_ = x if x_ is None else x_
        y_ = y if y_ is None else y_
        zh_ = zh if zh_ is None else zh_
        zlo_ = zlo if zlo_ is None else zlo_
        c_ = c if c_ is None else c_
        return (x_ * 16 + y_ * 4 + zh_, zlo_ * 2 + c_)

    def remote(src, dst, sid, rid, device):
        return pltpu.make_async_remote_copy(
            src_ref=src, dst_ref=dst, send_sem=ssem.at[sid], recv_sem=rsem.at[rid], device_id=device, device_id_type=MESH
        )

    def a_at(xb, q, r0=0, rows=TPD):
        return a_buf.at[pl.ds(pl.multiple_of(xb * TPD + r0, 16), rows), pl.ds(pl.multiple_of(q * FEAT, FEAT), FEAT)]

    def b_at(xw, yw, zw, n=1):
        return b_buf.at[pl.ds(pl.multiple_of(((xw * 4 + yw) * 4 + zw) * ROWS, ROWS), n * ROWS), :]

    def got(ref, rid):
        remote(ref, ref, 0, rid, dev(c_=1 - c)).wait_recv()

    def sent(ref, sid):
        remote(ref, ref, sid, 0, dev(c_=1 - c)).wait_send()

    def relay(ref, num, device):
        remote(ref, ref, num, num, device).start()

    load = pltpu.make_async_copy(tok, tv, rsem.at[TOK])
    load.start()

    barrier = pltpu.get_barrier_semaphore()
    for dx in range(4):
        for dc in range(2):
            if dx or dc:
                pl.semaphore_signal(barrier, inc=1, device_id=dev(x_=(x + dx) % 4, c_=(c + dc) % 2), device_id_type=MESH)
    for core in range(2):
        pl.semaphore_signal(barrier, inc=1, device_id=dev(zlo_=1 - zlo, c_=core), device_id_type=MESH)
    for other in (dev(y_=yp), dev(y_=ym), dev(zh_=zp), dev(zh_=zm)):
        pl.semaphore_signal(barrier, inc=1, device_id=other, device_id_type=MESH)

    kb = lax.broadcasted_iota(jnp.int32, (4, TPD), 1) // BLOCK
    qb = lax.broadcasted_iota(jnp.int32, (4, TPD), 0)
    for r in range(2):
        m = bm[r]
        seen = jnp.where(kb == 0, m[:, 0:1], jnp.where(kb == 1, m[:, 1:2], jnp.where(kb == 2, m[:, 2:3], m[:, 3:4])))
        mk[8 * r : 8 * r + 4, :] = jnp.where(jnp.logical_or(seen > 0, kb == qb), 1.0, 0.0)
        mk[8 * r + 4 : 8 * r + 8, :] = jnp.zeros((4, TPD), jnp.float32)
    mbuf[x] = mk[...]

    pl.semaphore_wait(barrier, 13)

    def swap(e, p, w):
        src = w.at[:, pl.ds(e * NC, NC)]
        here = b_at(x, y, zh).at[:, pl.ds(p * NC, NC)]
        away = jnp.logical_or(c + 2 * e != x, x // 2 != c)
        far = remote(src, here, SW + e, SW + x % 2, dev(x_=c + 2 * e, c_=x // 2))
        return away, far, pltpu.make_async_copy(src, here, rsem.at[SW + x % 2])

    for e in range(2):
        for p, w in enumerate((wq, wk, wv)):
            away, far, near = swap(e, p, w)

            @pl.when(away)
            def _():
                far.start()

            @pl.when(jnp.logical_not(away))
            def _():
                near.start()

    load.wait()
    lane = lax.broadcasted_iota(jnp.int32, (64, 128), 1)

    def stats(i, _):
        rr = pl.multiple_of(i * 64, 64)
        t1 = jnp.zeros((64, 128), jnp.float32)
        t2 = jnp.zeros((64, 128), jnp.float32)
        for j in range(FEAT // 128):
            v = tv[pl.ds(rr, 64), j * 128 : (j + 1) * 128].astype(jnp.float32)
            t1 = t1 + v
            t2 = t2 + v * v
        a1 = jnp.sum(t1, axis=-1, keepdims=True)
        a2 = jnp.sum(t2, axis=-1, keepdims=True)
        st[pl.ds(rr, 64), :] = jnp.where(lane == 0, a1, jnp.where(lane == 1, a2, 0.0))
        return 0

    lax.fori_loop(0, 8, stats, 0)
    for i in range(4):
        sg[t, :, i * 128 : (i + 1) * 128] = jnp.transpose(st[i * 128 : (i + 1) * 128, :])[:8]

    peers = [dev(c_=1 - c), dev(zlo_=1 - zlo), dev(zlo_=1 - zlo, c_=1 - c)]
    for k in range(3):
        remote(sg.at[t], sg.at[t], ST + k, ST + k, peers[k]).start()
    for k in range(3):
        remote(mk, mbuf.at[x], MK + k, MK + k, dev(x_=(x + k + 1) % 4)).start()
    theirs = [t + 1 - 2 * c, (t + 2) % 4, (t + 2) % 4 + 1 - 2 * c]
    for k in range(3):
        got(sg.at[theirs[k]], ST + k)
    total = (sg[0] + sg[1]) + (sg[2] + sg[3])
    mean = total[0:1] * (1.0 / D)
    rstd = lax.rsqrt(total[1:2] * (1.0 / D) - mean * mean + EPS)
    row = lax.broadcasted_iota(jnp.int32, (128, 128), 0)
    for i in range(4):
        cols = slice(i * 128, (i + 1) * 128)
        st[i * 128 : (i + 1) * 128, :] = jnp.transpose(jnp.where(row == 0, mean[:, cols], rstd[:, cols]))

    def norm(i, _):
        rr = pl.multiple_of(i * 64, 64)
        mu = jnp.broadcast_to(st[pl.ds(rr, 64), 0:1], (64, 128))
        rs = jnp.broadcast_to(st[pl.ds(rr, 64), 1:2], (64, 128))
        for j in range(FEAT // 128):
            v = tv[pl.ds(rr, 64), j * 128 : (j + 1) * 128].astype(jnp.float32)
            g = gn[:, pl.ds(pl.multiple_of(t * FEAT + j * 128, 128), 128)]
            nv[pl.ds(rr, 64), j * 128 : (j + 1) * 128] = ((v - mu) * rs * g).astype(jnp.bfloat16)
        return 0

    def first(r, dst_dev, base):
        return remote(nv.at[pl.ds(pl.multiple_of(r * TPD, TPD), TPD), :], a_at(x, t), base + r, base + c, dst_dev)

    turns = [c, 1 - c]
    for r in turns:
        lax.fori_loop(r * 4, r * 4 + 4, norm, 0)
        first(r, dev(x_=xp, c_=r), AXP).start()
        first(r, dev(x_=xm, c_=r), AXM).start()
    half = nv.at[pl.ds(pl.multiple_of((1 - c) * TPD, TPD), TPD), :]
    remote(half, a_at(x, t), AD, AD, dev(c_=1 - c)).start()
    own = pltpu.make_async_copy(nv.at[pl.ds(pl.multiple_of(c * TPD, TPD), TPD), :], a_at(x, t), rsem.at[AL])
    own.start()

    xw = [2 * c, 2 * c + 1]
    names = [zh, zm, zp, zo]

    def y_out(k, h):
        piece = b_at(xw[h], y, names[k])
        relay(piece, YP + 2 * k + h, dev(y_=yp))
        relay(piece, YM + 2 * k + h, dev(y_=ym))
        relay(piece, DO + 2 * k + h, dev(c_=1 - c))

    def y_on(k, h):
        got(b_at(xw[h], ym, names[k]), YP + 2 * k + h)
        if h == 0:
            relay(b_at(xw[0], ym, names[k]), YFP + k, dev(y_=yp))
        got(b_at(xw[h], yp, names[k]), YM + 2 * k + h)
        if h == 1:
            relay(b_at(xw[1], yp, names[k]), YFM + k, dev(y_=ym))

    for h in range(2):
        piece = b_at(xw[h], y, zh)
        got(piece, SW + h)
        relay(piece, ZP + h, dev(zh_=zp))
        relay(piece, ZM + h, dev(zh_=zm))
        y_out(0, h)

    acc[...] = jnp.zeros_like(acc)

    near_q = [2 * zlo + c, 2 * zlo + 1 - c]
    far_q = [2 * (1 - zlo) + c, 2 * (1 - zlo) + 1 - c]
    MID = TPD // 2

    def pair_on(part, plus, minus, r0, rows):
        piece = a_at(x, far_q[part], r0, rows)
        relay(piece, plus, dev(x_=xp))
        relay(piece, minus, dev(x_=xm))

    def order(i):
        return (x + jnp.where(i == 1, 3, jnp.where(i == 2, 1, jnp.where(i == 3, 2, 0)))) % 4

    def chunk(xb, half, yy):
        row = pl.multiple_of(xb * TPD, TPD)
        at = [pl.ds(pl.multiple_of(((2 * half + k) * 4 + yy) * 4 * ROWS, 128), 4 * ROWS) for k in range(2)]
        acc[pl.ds(row, TPD), :] += jnp.dot(
            jnp.concatenate([a_buf[pl.ds(row, TPD), at[k]] for k in range(2)], axis=1),
            jnp.concatenate([b_buf[at[k], :] for k in range(2)], axis=0),
            preferred_element_type=jnp.float32,
        )

    def beside(i):
        return (y + jnp.where(i == 1, 3, jnp.where(i == 2, 1, 0))) % 4

    def early(i, _):
        chunk(order(i), zlo, y)
        return 0

    def middle(i, _):
        chunk(order(i // 2), zlo, beside(1 + i % 2))
        return 0

    def opposite(i, _):
        chunk(xo, zlo, beside(i))
        return 0

    def across(i, _):
        chunk(x, 1 - zlo, beside(i))
        return 0

    def late(i, _):
        chunk(order(jnp.where(i == 4, 0, i)), jnp.where(i == 4, 1 - zlo, zlo), yo)
        return 0

    xv = [2 * (1 - c), 2 * (1 - c) + 1]
    y_on(0, 0)
    got(b_at(xw[0], y, zm), ZP)
    relay(b_at(xw[0], y, zm), ZFP, dev(zh_=zp))
    y_out(1, 0)
    got(b_at(xw[0], y, zp), ZM)
    y_out(2, 0)
    y_on(0, 1)
    got(b_at(xw[1], y, zm), ZP + 1)
    y_out(1, 1)
    got(b_at(xw[1], y, zp), ZM + 1)
    relay(b_at(xw[1], y, zp), ZFM, dev(zh_=zm))
    y_out(2, 1)
    y_on(1, 0)
    y_on(2, 0)
    got(b_at(xw[0], y, zo), ZFP)
    for r in turns:
        first(r, dev(zlo_=1 - zlo, c_=r), AZ).start()
    y_out(3, 0)
    got(b_at(xw[1], y, zo), ZFM)
    y_out(3, 1)
    def ahead(part, plus, minus, core):
        got(a_at(xm, near_q[part]), AXP + core)
        relay(a_at(xm, near_q[part], 0, MID), plus, dev(x_=xp))
        got(a_at(xp, near_q[part]), AXM + core)
        relay(a_at(xp, near_q[part], MID, MID), minus, dev(x_=xm))

    ahead(0, AOP, AOM, c)
    y_on(1, 1)
    y_on(2, 1)
    ahead(1, AQP, AQM, 1 - c)
    for h in range(2):
        for k in range(4):
            got(b_at(xv[h], y, names[k]), DO + 2 * k + h)
    got(a_at(x, 2 * zlo + 1 - c), AD)
    own.wait()
    lax.fori_loop(0, 3, early, 0)
    got(a_at(x, far_q[0]), AZ + c)
    pair_on(0, AIIP, AIIM, 0, TPD)
    y_on(3, 0)
    y_on(3, 1)
    for base, yy in ((DYM, ym), (DYP, yp)):
        for h in range(2):
            relay(b_at(xw[h], yy, 0, 4), base + h, dev(c_=1 - c))
    got(a_at(xo, near_q[0], 0, MID), AOP)
    relay(a_at(xo, near_q[0], 0, TPD - 2 * BYX), AIII, dev(zlo_=1 - zlo))
    got(a_at(xo, near_q[1], 0, MID), AQP)
    relay(a_at(xo, near_q[1], 0, MID), AIII + 1, dev(zlo_=1 - zlo))
    got(a_at(xo, near_q[1], MID, MID), AQM)
    relay(a_at(xo, near_q[1], MID, MID), AIV, dev(zlo_=1 - zlo))
    for base, yy in ((DYM, ym), (DYP, yp)):
        for h in range(2):
            got(b_at(xv[h], yy, 0, 4), base + h)
    lax.fori_loop(0, 6, middle, 0)
    got(a_at(x, far_q[1]), AZ + 1 - c)
    pair_on(1, AIIP + 1, AIIM + 1, 0, MID)
    got(a_at(xo, near_q[0], MID, MID), AOM)
    lax.fori_loop(0, 3, opposite, 0)
    for h, num in enumerate((YFP, YFM)):
        for k in range(4):
            got(b_at(xw[h], yo, names[k]), num + k)
        relay(b_at(xw[h], yo, 0, 4), DYO + h, dev(c_=1 - c))
    got(a_at(xm, far_q[0]), AIIP)
    relay(a_at(xm, far_q[0], TPD - 2 * BYX, BYX), AFP, dev(x_=xp))
    got(a_at(xp, far_q[0]), AIIM)
    relay(a_at(xp, far_q[0], TPD - BYX, BYX), AFM, dev(x_=xm))
    pair_on(1, ALP, ALM, MID, MID)
    lax.fori_loop(0, 3, across, 0)
    for h in range(2):
        got(b_at(xv[h], yo, 0, 4), DYO + h)
    lax.fori_loop(0, 5, late, 0)
    for k in range(3):
        got(mbuf.at[(x + 3 - k) % 4], MK + k)

    def unit(xb, q, r0=0, n=TPD):
        row = pl.multiple_of(xb * TPD + r0, MID)
        col = pl.multiple_of(q * FEAT, FEAT)
        acc[pl.ds(row, n), :] += jnp.dot(
            a_buf[pl.ds(row, n), pl.ds(col, FEAT)], b_buf[pl.ds(col, FEAT), :], preferred_element_type=jnp.float32
        )

    def out_copy(xb, i, j):
        src = obuf.at[i, :, pl.ds(j * DH, DH)]
        cols = pl.ds(pl.multiple_of((x // 2) * NC + j * DH, DH), DH)
        dst = out.at[pl.ds(pl.multiple_of(c * TPD, TPD), TPD), cols]
        rid = OUT + 2 * (x // 2) + c
        return remote(src, dst, OUT + i, rid, dev(x_=xb, c_=x % 2)), pltpu.make_async_copy(src, dst, rsem.at[rid])

    def goes(xb):
        return jnp.logical_or(xb != x, x % 2 != c)

    def finish(i):
        xb = order(i)
        row = pl.multiple_of(xb * TPD, TPD)

        def part(p, j):
            return acc[pl.ds(row, TPD), p * NC + j * DH : p * NC + (j + 1) * DH]

        def head_norm(values, gain):
            ms = jnp.mean(values * values, axis=-1, keepdims=True)
            return (values * lax.rsqrt(ms + EPS) * gain).astype(jnp.bfloat16)

        allowed = mbuf[xb]
        seen = jnp.concatenate(
            [jnp.broadcast_to(jnp.where(c == 0, allowed[b : b + 1], allowed[8 + b : 9 + b]), (BLOCK, TPD)) for b in range(4)], axis=0
        )
        for j in range(3):
            qn = head_norm(part(0, j), qg[...])
            kn = head_norm(part(1, j), kg[...])
            v = part(2, j).astype(jnp.bfloat16)
            s = lax.dot_general(qn, kn, (((1,), (1,)), ((), ())), preferred_element_type=jnp.float32) * (1.0 / DH**0.5)
            s = jnp.where(seen > 0, s, jnp.float32(-1e30))
            w = jnp.exp(s - jnp.max(s, axis=-1, keepdims=True))
            probs = (w / jnp.sum(w, axis=-1, keepdims=True)).astype(jnp.bfloat16)
            obuf[i, :, j * DH : (j + 1) * DH] = jnp.dot(probs, v, preferred_element_type=jnp.float32).astype(jnp.bfloat16)
            far, near_ = out_copy(xb, i, j)

            @pl.when(goes(xb))
            def _():
                far.start()

            @pl.when(jnp.logical_not(goes(xb)))
            def _():
                near_.start()

    finish(0)

    def third(i, _):
        @pl.when(i == 3)
        def _():
            got(a_at(xo, far_q[0], 0, TPD - 2 * BYX), AIII)
            got(a_at(xo, far_q[0], TPD - 2 * BYX, BYX), AFP)
            got(a_at(xo, far_q[0], TPD - BYX, BYX), AFM)

        unit(order(i), far_q[0])
        return 0

    lax.fori_loop(1, 4, third, 0)

    def upper(i, _):
        for k, (num, blk) in enumerate(((AIIP, xm), (AIIM, xp))):

            @pl.when(i == k + 1)
            def _():
                got(a_at(blk, far_q[1], 0, MID), num + 1)

        unit(order(i), far_q[1], 0, MID)
        return 0

    lax.fori_loop(1, 3, upper, 0)

    got(a_at(xo, far_q[1], 0, MID), AIII + 1)
    got(a_at(xo, far_q[1], MID, MID), AIV)
    unit(xo, far_q[1])
    finish(3)

    def last(i, _):
        for k, (num, blk) in enumerate(((ALP, xm), (ALM, xp))):

            @pl.when(i == k + 1)
            def _():
                got(a_at(blk, far_q[1], MID, MID), num)

        unit(order(i), far_q[1], MID, MID)
        finish(i)
        return 0

    lax.fori_loop(1, 3, last, 0)

    for e in range(2):
        for r in range(2):
            got(out.at[pl.ds(r * TPD, TPD), pl.ds(e * NC, NC)], OUT + 2 * e + r)
    for num in (AXP, AXP + 1, AXM, AXM + 1, AD, AIIP, AIIM):
        sent(a_at(x, t), num)
    sent(a_at(x, t, 0, TPD - 2 * BYX), AIII)
    for num in (AOP, AOM, AQP, AQM, AIII + 1, AIV, AIIP + 1, AIIM + 1, ALP, ALM):
        sent(a_at(x, t, 0, MID), num)
    for r in range(2):
        sent(a_at(x, t), AZ + r)
    for num in (AFP, AFM):
        sent(a_at(x, t, 0, BYX), num)
    for k in range(3):
        sent(mk, MK + k)
        sent(sg.at[t], ST + k)
    for e in range(2):

        @pl.when(jnp.logical_or(c + 2 * e != x, x // 2 != c))
        def _():
            sent(b_at(x, y, zh), SW + e)

    for num in range(ZP, DYM):
        sent(b_at(x, y, zh), num)
    for num in range(DYM, OUT):
        sent(b_at(x, y, 0, 4), num)
    for i in range(4):

        @pl.when(goes(order(i)))
        def _():
            sent(obuf.at[i], OUT + i)


def per_device(tokens, block_mask, norm_gain, w_query, w_key, w_value, query_gain, key_gain):
    vmem = pl.BlockSpec(memory_space=pltpu.VMEM)
    hbm = pl.BlockSpec(memory_space=pl.ANY)
    return pl.pallas_call(
        kernel,
        out_shape=pltpu.VMEM((512, 768), jnp.bfloat16),
        in_specs=[hbm, vmem, vmem, hbm, hbm, hbm, vmem, vmem],
        out_specs=vmem,
        scratch_shapes=[
            pltpu.VMEM((2 * TPD, FEAT), jnp.bfloat16),
            pltpu.VMEM((2 * TPD, FEAT), jnp.bfloat16),
            pltpu.VMEM((2 * TPD, 128), jnp.float32),
            pltpu.VMEM((4, 8, 2 * TPD), jnp.float32),
            pltpu.VMEM((4 * TPD, D), jnp.bfloat16),
            pltpu.VMEM((D, N), jnp.bfloat16),
            pltpu.VMEM((4 * TPD, N), jnp.float32),
            pltpu.VMEM((16, TPD), jnp.float32),
            pltpu.VMEM((4, 16, TPD), jnp.float32),
            pltpu.VMEM((4, TPD, NC), jnp.bfloat16),
            pltpu.SemaphoreType.DMA((COUNT,)),
            pltpu.SemaphoreType.DMA((COUNT,)),
        ],
        compiler_params=pltpu.CompilerParams(collective_id=0, has_side_effects=True, vmem_limit_bytes=60 << 20),
    )(tokens, block_mask, norm_gain.reshape(1, D), w_query, w_key, w_value, query_gain.reshape(1, DH), key_gain.reshape(1, DH))


def solution(mesh):
    return jax.shard_map(
        per_device,
        mesh=mesh,
        in_specs=(
            P("dp", "tensor"),
            P("dp", None, None),
            P(),
            P("dp", "tensor"),
            P("dp", "tensor"),
            P("dp", "tensor"),
            P(),
            P(),
        ),
        out_specs=P("dp", "tensor"),
        check_vma=False,
    )
```

```python
import jax
import jax.numpy as jnp
from jax import lax
from jax.experimental import pallas as pl
from jax.experimental.pallas import tpu as pltpu
from jax.sharding import PartitionSpec as P

DH = 128
TPD = 256
BLOCK = 64
EPS = 1e-06
MESH = pl.DeviceIdType.MESH

ROWS = 96
FEAT = 1536
D = 6144
NC = 384
N = 3 * NC

AXP, AXM, AZ = 0, 2, 4
AD, AL, AOP, AOM = 8, 9, 10, 11
AIIP, AIIM, AIII = 12, 14, 16
AFP, AFM = 18, 19
MK = 20
ST = 23
SW = 26
ZP, ZM, ZFP, ZFM = 28, 30, 32, 33
YP, YM = 34, 42
YFP, YFM = 50, 54
DO = 58
DYM, DYP, DYO = 66, 68, 70
OUT = 72
TOK = 76
ALP, ALM = 77, 78
AQP, AQM, AIV = 79, 80, 81
COUNT = 82
BP, BM = 64, 128
BZ = TPD - BP - BM


def kernel(
    tok, bm, gn, wq, wk, wv, qg, kg, out, tv, nv, st, sg, a_buf, b_buf, acc, mk, mbuf, obuf, ssem, rsem
):
    dp = lax.axis_index("dp")
    t = lax.axis_index("tensor")
    x, y, zh = dp // 16, (dp // 4) % 4, dp % 4
    zlo, c = t // 2, t % 2
    xp, xm, xo = (x + 1) % 4, (x + 3) % 4, (x + 2) % 4
    yp, ym, yo = (y + 1) % 4, (y + 3) % 4, (y + 2) % 4
    zp, zm, zo = (zh + 1) % 4, (zh + 3) % 4, (zh + 2) % 4

    def dev(x_=None, y_=None, zh_=None, zlo_=None, c_=None):
        x_ = x if x_ is None else x_
        y_ = y if y_ is None else y_
        zh_ = zh if zh_ is None else zh_
        zlo_ = zlo if zlo_ is None else zlo_
        c_ = c if c_ is None else c_
        return (x_ * 16 + y_ * 4 + zh_, zlo_ * 2 + c_)

    def remote(src, dst, sid, rid, device):
        return pltpu.make_async_remote_copy(
            src_ref=src, dst_ref=dst, send_sem=ssem.at[sid], recv_sem=rsem.at[rid], device_id=device, device_id_type=MESH
        )

    def a_at(xb, q, r0=0, rows=TPD):
        return a_buf.at[pl.ds(pl.multiple_of(xb * TPD + r0, 16), rows), pl.ds(pl.multiple_of(q * FEAT, FEAT), FEAT)]

    def b_at(xw, yw, zw, n=1):
        return b_buf.at[pl.ds(pl.multiple_of(((xw * 4 + yw) * 4 + zw) * ROWS, ROWS), n * ROWS), :]

    def got(ref, rid):
        remote(ref, ref, 0, rid, dev(c_=1 - c)).wait_recv()

    def sent(ref, sid):
        remote(ref, ref, sid, 0, dev(c_=1 - c)).wait_send()

    def relay(ref, num, device):
        remote(ref, ref, num, num, device).start()

    load = pltpu.make_async_copy(tok, tv, rsem.at[TOK])
    load.start()

    barrier = pltpu.get_barrier_semaphore()
    for dx in range(4):
        for dc in range(2):
            if dx or dc:
                pl.semaphore_signal(barrier, inc=1, device_id=dev(x_=(x + dx) % 4, c_=(c + dc) % 2), device_id_type=MESH)
    for core in range(2):
        pl.semaphore_signal(barrier, inc=1, device_id=dev(zlo_=1 - zlo, c_=core), device_id_type=MESH)
    for other in (dev(y_=yp), dev(y_=ym), dev(zh_=zp), dev(zh_=zm)):
        pl.semaphore_signal(barrier, inc=1, device_id=other, device_id_type=MESH)

    kb = lax.broadcasted_iota(jnp.int32, (4, TPD), 1) // BLOCK
    qb = lax.broadcasted_iota(jnp.int32, (4, TPD), 0)
    for r in range(2):
        m = bm[r]
        seen = jnp.where(kb == 0, m[:, 0:1], jnp.where(kb == 1, m[:, 1:2], jnp.where(kb == 2, m[:, 2:3], m[:, 3:4])))
        mk[8 * r : 8 * r + 4, :] = jnp.where(jnp.logical_or(seen > 0, kb == qb), 1.0, 0.0)
        mk[8 * r + 4 : 8 * r + 8, :] = jnp.zeros((4, TPD), jnp.float32)
    mbuf[x] = mk[...]

    pl.semaphore_wait(barrier, 13)

    def swap(e, p, w):
        src = w.at[:, pl.ds(e * NC, NC)]
        here = b_at(x, y, zh).at[:, pl.ds(p * NC, NC)]
        away = jnp.logical_or(c + 2 * e != x, x // 2 != c)
        far = remote(src, here, SW + e, SW + x % 2, dev(x_=c + 2 * e, c_=x // 2))
        return away, far, pltpu.make_async_copy(src, here, rsem.at[SW + x % 2])

    for e in range(2):
        for p, w in enumerate((wq, wk, wv)):
            away, far, near = swap(e, p, w)

            @pl.when(away)
            def _():
                far.start()

            @pl.when(jnp.logical_not(away))
            def _():
                near.start()

    load.wait()
    lane = lax.broadcasted_iota(jnp.int32, (64, 128), 1)

    def stats(i, _):
        rr = pl.multiple_of(i * 64, 64)
        t1 = jnp.zeros((64, 128), jnp.float32)
        t2 = jnp.zeros((64, 128), jnp.float32)
        for j in range(FEAT // 128):
            v = tv[pl.ds(rr, 64), j * 128 : (j + 1) * 128].astype(jnp.float32)
            t1 = t1 + v
            t2 = t2 + v * v
        a1 = jnp.sum(t1, axis=-1, keepdims=True)
        a2 = jnp.sum(t2, axis=-1, keepdims=True)
        st[pl.ds(rr, 64), :] = jnp.where(lane == 0, a1, jnp.where(lane == 1, a2, 0.0))
        return 0

    lax.fori_loop(0, 8, stats, 0)
    for i in range(4):
        sg[t, :, i * 128 : (i + 1) * 128] = jnp.transpose(st[i * 128 : (i + 1) * 128, :])[:8]

    peers = [dev(c_=1 - c), dev(zlo_=1 - zlo), dev(zlo_=1 - zlo, c_=1 - c)]
    for k in range(3):
        remote(sg.at[t], sg.at[t], ST + k, ST + k, peers[k]).start()
    for k in range(3):
        remote(mk, mbuf.at[x], MK + k, MK + k, dev(x_=(x + k + 1) % 4)).start()
    theirs = [t + 1 - 2 * c, (t + 2) % 4, (t + 2) % 4 + 1 - 2 * c]
    for k in range(3):
        got(sg.at[theirs[k]], ST + k)
    total = (sg[0] + sg[1]) + (sg[2] + sg[3])
    mean = total[0:1] * (1.0 / D)
    rstd = lax.rsqrt(total[1:2] * (1.0 / D) - mean * mean + EPS)
    row = lax.broadcasted_iota(jnp.int32, (128, 128), 0)
    for i in range(4):
        cols = slice(i * 128, (i + 1) * 128)
        st[i * 128 : (i + 1) * 128, :] = jnp.transpose(jnp.where(row == 0, mean[:, cols], rstd[:, cols]))

    def norm(i, _):
        rr = pl.multiple_of(i * 64, 64)
        mu = jnp.broadcast_to(st[pl.ds(rr, 64), 0:1], (64, 128))
        rs = jnp.broadcast_to(st[pl.ds(rr, 64), 1:2], (64, 128))
        for j in range(FEAT // 128):
            v = tv[pl.ds(rr, 64), j * 128 : (j + 1) * 128].astype(jnp.float32)
            g = gn[:, pl.ds(pl.multiple_of(t * FEAT + j * 128, 128), 128)]
            nv[pl.ds(rr, 64), j * 128 : (j + 1) * 128] = ((v - mu) * rs * g).astype(jnp.bfloat16)
        return 0

    def first(r, dst_dev, base):
        return remote(nv.at[pl.ds(pl.multiple_of(r * TPD, TPD), TPD), :], a_at(x, t), base + r, base + c, dst_dev)

    turns = [c, 1 - c]
    for r in turns:
        lax.fori_loop(r * 4, r * 4 + 4, norm, 0)
        first(r, dev(x_=xp, c_=r), AXP).start()
        first(r, dev(x_=xm, c_=r), AXM).start()
    half = nv.at[pl.ds(pl.multiple_of((1 - c) * TPD, TPD), TPD), :]
    remote(half, a_at(x, t), AD, AD, dev(c_=1 - c)).start()
    own = pltpu.make_async_copy(nv.at[pl.ds(pl.multiple_of(c * TPD, TPD), TPD), :], a_at(x, t), rsem.at[AL])
    own.start()

    xw = [2 * c, 2 * c + 1]
    names = [zh, zm, zp, zo]

    def y_out(k, h):
        piece = b_at(xw[h], y, names[k])
        relay(piece, YP + 2 * k + h, dev(y_=yp))
        relay(piece, YM + 2 * k + h, dev(y_=ym))
        relay(piece, DO + 2 * k + h, dev(c_=1 - c))

    def y_on(k, h):
        got(b_at(xw[h], ym, names[k]), YP + 2 * k + h)
        if h == 0:
            relay(b_at(xw[0], ym, names[k]), YFP + k, dev(y_=yp))
        got(b_at(xw[h], yp, names[k]), YM + 2 * k + h)
        if h == 1:
            relay(b_at(xw[1], yp, names[k]), YFM + k, dev(y_=ym))

    for h in range(2):
        piece = b_at(xw[h], y, zh)
        got(piece, SW + h)
        relay(piece, ZP + h, dev(zh_=zp))
        relay(piece, ZM + h, dev(zh_=zm))
        y_out(0, h)

    acc[...] = jnp.zeros_like(acc)

    near_q = [2 * zlo + c, 2 * zlo + 1 - c]
    far_q = [2 * (1 - zlo) + c, 2 * (1 - zlo) + 1 - c]
    MID = TPD // 2

    def pair_on(part, plus, minus, r0, rows):
        piece = a_at(x, far_q[part], r0, rows)
        relay(piece, plus, dev(x_=xp))
        relay(piece, minus, dev(x_=xm))

    def order(i):
        return (x + jnp.where(i == 1, 3, jnp.where(i == 2, 1, jnp.where(i == 3, 2, 0)))) % 4

    def chunk(xb, half, yy):
        row = pl.multiple_of(xb * TPD, TPD)
        at = [pl.ds(pl.multiple_of(((2 * half + k) * 4 + yy) * 4 * ROWS, 128), 4 * ROWS) for k in range(2)]
        acc[pl.ds(row, TPD), :] += jnp.dot(
            jnp.concatenate([a_buf[pl.ds(row, TPD), at[k]] for k in range(2)], axis=1),
            jnp.concatenate([b_buf[at[k], :] for k in range(2)], axis=0),
            preferred_element_type=jnp.float32,
        )

    def beside(i):
        return (y + jnp.where(i == 1, 3, jnp.where(i == 2, 1, 0))) % 4

    def early(i, _):
        chunk(order(i), zlo, y)
        return 0

    def middle(i, _):
        chunk(order(i // 2), zlo, beside(1 + i % 2))
        return 0

    def opposite(i, _):
        chunk(xo, zlo, beside(i))
        return 0

    def across(i, _):
        chunk(x, 1 - zlo, beside(i))
        return 0

    def late(i, _):
        chunk(order(jnp.where(i == 4, 0, i)), jnp.where(i == 4, 1 - zlo, zlo), yo)
        return 0

    xv = [2 * (1 - c), 2 * (1 - c) + 1]
    y_on(0, 0)
    got(b_at(xw[0], y, zm), ZP)
    relay(b_at(xw[0], y, zm), ZFP, dev(zh_=zp))
    y_out(1, 0)
    got(b_at(xw[0], y, zp), ZM)
    y_out(2, 0)
    y_on(0, 1)
    got(b_at(xw[1], y, zm), ZP + 1)
    y_out(1, 1)
    got(b_at(xw[1], y, zp), ZM + 1)
    relay(b_at(xw[1], y, zp), ZFM, dev(zh_=zm))
    y_out(2, 1)
    y_on(1, 0)
    y_on(2, 0)
    got(b_at(xw[0], y, zo), ZFP)
    for r in turns:
        first(r, dev(zlo_=1 - zlo, c_=r), AZ).start()
    y_out(3, 0)
    got(b_at(xw[1], y, zo), ZFM)
    y_out(3, 1)
    def ahead(part, plus, minus, core):
        got(a_at(xm, near_q[part]), AXP + core)
        relay(a_at(xm, near_q[part], 0, MID), plus, dev(x_=xp))
        got(a_at(xp, near_q[part]), AXM + core)
        relay(a_at(xp, near_q[part], MID, MID), minus, dev(x_=xm))

    ahead(0, AOP, AOM, c)
    y_on(1, 1)
    y_on(2, 1)
    ahead(1, AQP, AQM, 1 - c)
    for h in range(2):
        for k in range(4):
            got(b_at(xv[h], y, names[k]), DO + 2 * k + h)
    got(a_at(x, 2 * zlo + 1 - c), AD)
    own.wait()
    lax.fori_loop(0, 3, early, 0)
    got(a_at(x, far_q[0]), AZ + c)
    pair_on(0, AIIP, AIIM, 0, TPD)
    y_on(3, 0)
    y_on(3, 1)
    for base, yy in ((DYM, ym), (DYP, yp)):
        for h in range(2):
            relay(b_at(xw[h], yy, 0, 4), base + h, dev(c_=1 - c))
    got(a_at(xo, near_q[0], 0, MID), AOP)
    relay(a_at(xo, near_q[0], 0, BZ), AIII, dev(zlo_=1 - zlo))
    got(a_at(xo, near_q[1], 0, MID), AQP)
    relay(a_at(xo, near_q[1], 0, MID), AIII + 1, dev(zlo_=1 - zlo))
    got(a_at(xo, near_q[1], MID, MID), AQM)
    relay(a_at(xo, near_q[1], MID, MID), AIV, dev(zlo_=1 - zlo))
    for base, yy in ((DYM, ym), (DYP, yp)):
        for h in range(2):
            got(b_at(xv[h], yy, 0, 4), base + h)
    lax.fori_loop(0, 6, middle, 0)
    got(a_at(x, far_q[1]), AZ + 1 - c)
    pair_on(1, AIIP + 1, AIIM + 1, 0, MID)
    got(a_at(xo, near_q[0], MID, MID), AOM)
    lax.fori_loop(0, 3, opposite, 0)
    for h, num in enumerate((YFP, YFM)):
        for k in range(4):
            got(b_at(xw[h], yo, names[k]), num + k)
        relay(b_at(xw[h], yo, 0, 4), DYO + h, dev(c_=1 - c))
    got(a_at(xm, far_q[0]), AIIP)
    relay(a_at(xm, far_q[0], BZ, BP), AFP, dev(x_=xp))
    got(a_at(xp, far_q[0]), AIIM)
    relay(a_at(xp, far_q[0], BZ + BP, BM), AFM, dev(x_=xm))
    pair_on(1, ALP, ALM, MID, MID)
    lax.fori_loop(0, 3, across, 0)
    for h in range(2):
        got(b_at(xv[h], yo, 0, 4), DYO + h)
    lax.fori_loop(0, 5, late, 0)
    for k in range(3):
        got(mbuf.at[(x + 3 - k) % 4], MK + k)

    def unit(xb, q, r0=0, n=TPD):
        row = pl.multiple_of(xb * TPD + r0, MID)
        col = pl.multiple_of(q * FEAT, FEAT)
        acc[pl.ds(row, n), :] += jnp.dot(
            a_buf[pl.ds(row, n), pl.ds(col, FEAT)], b_buf[pl.ds(col, FEAT), :], preferred_element_type=jnp.float32
        )

    def out_copy(xb, i, j):
        src = obuf.at[i, :, pl.ds(j * DH, DH)]
        cols = pl.ds(pl.multiple_of((x // 2) * NC + j * DH, DH), DH)
        dst = out.at[pl.ds(pl.multiple_of(c * TPD, TPD), TPD), cols]
        rid = OUT + 2 * (x // 2) + c
        return remote(src, dst, OUT + i, rid, dev(x_=xb, c_=x % 2)), pltpu.make_async_copy(src, dst, rsem.at[rid])

    def goes(xb):
        return jnp.logical_or(xb != x, x % 2 != c)

    def finish(i):
        xb = order(i)
        row = pl.multiple_of(xb * TPD, TPD)

        def part(p, j):
            return acc[pl.ds(row, TPD), p * NC + j * DH : p * NC + (j + 1) * DH]

        def head_norm(values, gain):
            ms = jnp.mean(values * values, axis=-1, keepdims=True)
            return (values * lax.rsqrt(ms + EPS) * gain).astype(jnp.bfloat16)

        allowed = mbuf[xb]
        seen = jnp.concatenate(
            [jnp.broadcast_to(jnp.where(c == 0, allowed[b : b + 1], allowed[8 + b : 9 + b]), (BLOCK, TPD)) for b in range(4)], axis=0
        )
        for j in range(3):
            qn = head_norm(part(0, j), qg[...])
            kn = head_norm(part(1, j), kg[...])
            v = part(2, j).astype(jnp.bfloat16)
            s = lax.dot_general(qn, kn, (((1,), (1,)), ((), ())), preferred_element_type=jnp.float32) * (1.0 / DH**0.5)
            s = jnp.where(seen > 0, s, jnp.float32(-1e30))
            w = jnp.exp(s - jnp.max(s, axis=-1, keepdims=True))
            probs = (w / jnp.sum(w, axis=-1, keepdims=True)).astype(jnp.bfloat16)
            obuf[i, :, j * DH : (j + 1) * DH] = jnp.dot(probs, v, preferred_element_type=jnp.float32).astype(jnp.bfloat16)
            far, near_ = out_copy(xb, i, j)

            @pl.when(goes(xb))
            def _():
                far.start()

            @pl.when(jnp.logical_not(goes(xb)))
            def _():
                near_.start()

    finish(0)

    def third(i, _):
        @pl.when(i == 3)
        def _():
            got(a_at(xo, far_q[0], 0, BZ), AIII)
            got(a_at(xo, far_q[0], BZ, BP), AFP)
            got(a_at(xo, far_q[0], BZ + BP, BM), AFM)

        unit(order(i), far_q[0])
        return 0

    lax.fori_loop(1, 4, third, 0)

    def upper(i, _):
        for k, (num, blk) in enumerate(((AIIP, xm), (AIIM, xp))):

            @pl.when(i == k + 1)
            def _():
                got(a_at(blk, far_q[1], 0, MID), num + 1)

        unit(order(i), far_q[1], 0, MID)
        return 0

    lax.fori_loop(1, 3, upper, 0)

    got(a_at(xo, far_q[1], 0, MID), AIII + 1)
    got(a_at(xo, far_q[1], MID, MID), AIV)
    unit(xo, far_q[1])
    finish(3)

    def last(i, _):
        for k, (num, blk) in enumerate(((ALP, xm), (ALM, xp))):

            @pl.when(i == k + 1)
            def _():
                got(a_at(blk, far_q[1], MID, MID), num)

        unit(order(i), far_q[1], MID, MID)
        finish(i)
        return 0

    lax.fori_loop(1, 3, last, 0)

    for e in range(2):
        for r in range(2):
            got(out.at[pl.ds(r * TPD, TPD), pl.ds(e * NC, NC)], OUT + 2 * e + r)
    for num in (AXP, AXP + 1, AXM, AXM + 1, AD, AIIP, AIIM):
        sent(a_at(x, t), num)
    sent(a_at(x, t, 0, BZ), AIII)
    for num in (AOP, AOM, AQP, AQM, AIII + 1, AIV, AIIP + 1, AIIM + 1, ALP, ALM):
        sent(a_at(x, t, 0, MID), num)
    for r in range(2):
        sent(a_at(x, t), AZ + r)
    sent(a_at(x, t, 0, BP), AFP)
    sent(a_at(x, t, 0, BM), AFM)
    for k in range(3):
        sent(mk, MK + k)
        sent(sg.at[t], ST + k)
    for e in range(2):

        @pl.when(jnp.logical_or(c + 2 * e != x, x // 2 != c))
        def _():
            sent(b_at(x, y, zh), SW + e)

    for num in range(ZP, DYM):
        sent(b_at(x, y, zh), num)
    for num in range(DYM, OUT):
        sent(b_at(x, y, 0, 4), num)
    for i in range(4):

        @pl.when(goes(order(i)))
        def _():
            sent(obuf.at[i], OUT + i)


def per_device(tokens, block_mask, norm_gain, w_query, w_key, w_value, query_gain, key_gain):
    vmem = pl.BlockSpec(memory_space=pltpu.VMEM)
    hbm = pl.BlockSpec(memory_space=pl.ANY)
    return pl.pallas_call(
        kernel,
        out_shape=pltpu.VMEM((512, 768), jnp.bfloat16),
        in_specs=[hbm, vmem, vmem, hbm, hbm, hbm, vmem, vmem],
        out_specs=vmem,
        scratch_shapes=[
            pltpu.VMEM((2 * TPD, FEAT), jnp.bfloat16),
            pltpu.VMEM((2 * TPD, FEAT), jnp.bfloat16),
            pltpu.VMEM((2 * TPD, 128), jnp.float32),
            pltpu.VMEM((4, 8, 2 * TPD), jnp.float32),
            pltpu.VMEM((4 * TPD, D), jnp.bfloat16),
            pltpu.VMEM((D, N), jnp.bfloat16),
            pltpu.VMEM((4 * TPD, N), jnp.float32),
            pltpu.VMEM((16, TPD), jnp.float32),
            pltpu.VMEM((4, 16, TPD), jnp.float32),
            pltpu.VMEM((4, TPD, NC), jnp.bfloat16),
            pltpu.SemaphoreType.DMA((COUNT,)),
            pltpu.SemaphoreType.DMA((COUNT,)),
        ],
        compiler_params=pltpu.CompilerParams(collective_id=0, has_side_effects=True, vmem_limit_bytes=60 << 20),
    )(tokens, block_mask, norm_gain.reshape(1, D), w_query, w_key, w_value, query_gain.reshape(1, DH), key_gain.reshape(1, DH))


def solution(mesh):
    return jax.shard_map(
        per_device,
        mesh=mesh,
        in_specs=(
            P("dp", "tensor"),
            P("dp", None, None),
            P(),
            P("dp", "tensor"),
            P("dp", "tensor"),
            P("dp", "tensor"),
            P(),
            P(),
        ),
        out_specs=P("dp", "tensor"),
        check_vma=False,
    )
```

```python
import jax
import jax.numpy as jnp
from jax import lax
from jax.experimental import pallas as pl
from jax.experimental.pallas import tpu as pltpu
from jax.sharding import PartitionSpec as P

DH = 128
TPD = 256
BLOCK = 64
EPS = 1e-06
MESH = pl.DeviceIdType.MESH

ROWS = 96
FEAT = 1536
D = 6144
NC = 384
N = 3 * NC

AXP, AXM, AZ = 0, 2, 4
AD, AL, AOP, AOM = 8, 9, 10, 11
AIIP, AIIM, AIII = 12, 14, 16
AFP, AFM = 18, 19
MK = 20
ST = 23
SW = 26
ZP, ZM, ZFP, ZFM = 28, 30, 32, 33
YP, YM = 34, 42
YFP, YFM = 50, 54
DO = 58
DYM, DYP, DYO = 66, 68, 70
OUT = 72
TOK = 76
ALP, ALM = 77, 78
AQP, AQM, AIV = 79, 80, 81
COUNT = 82
BP, BM = 64, 112
BZ = TPD - BP - BM


def kernel(
    tok, bm, gn, wq, wk, wv, qg, kg, out, tv, nv, st, sg, a_buf, b_buf, acc, mk, mbuf, obuf, ssem, rsem
):
    dp = lax.axis_index("dp")
    t = lax.axis_index("tensor")
    x, y, zh = dp // 16, (dp // 4) % 4, dp % 4
    zlo, c = t // 2, t % 2
    xp, xm, xo = (x + 1) % 4, (x + 3) % 4, (x + 2) % 4
    yp, ym, yo = (y + 1) % 4, (y + 3) % 4, (y + 2) % 4
    zp, zm, zo = (zh + 1) % 4, (zh + 3) % 4, (zh + 2) % 4

    def dev(x_=None, y_=None, zh_=None, zlo_=None, c_=None):
        x_ = x if x_ is None else x_
        y_ = y if y_ is None else y_
        zh_ = zh if zh_ is None else zh_
        zlo_ = zlo if zlo_ is None else zlo_
        c_ = c if c_ is None else c_
        return (x_ * 16 + y_ * 4 + zh_, zlo_ * 2 + c_)

    def remote(src, dst, sid, rid, device):
        return pltpu.make_async_remote_copy(
            src_ref=src, dst_ref=dst, send_sem=ssem.at[sid], recv_sem=rsem.at[rid], device_id=device, device_id_type=MESH
        )

    def a_at(xb, q, r0=0, rows=TPD):
        return a_buf.at[pl.ds(pl.multiple_of(xb * TPD + r0, 16), rows), pl.ds(pl.multiple_of(q * FEAT, FEAT), FEAT)]

    def b_at(xw, yw, zw, n=1):
        return b_buf.at[pl.ds(pl.multiple_of(((xw * 4 + yw) * 4 + zw) * ROWS, ROWS), n * ROWS), :]

    def got(ref, rid):
        remote(ref, ref, 0, rid, dev(c_=1 - c)).wait_recv()

    def sent(ref, sid):
        remote(ref, ref, sid, 0, dev(c_=1 - c)).wait_send()

    def relay(ref, num, device):
        remote(ref, ref, num, num, device).start()

    load = pltpu.make_async_copy(tok, tv, rsem.at[TOK])
    load.start()

    barrier = pltpu.get_barrier_semaphore()
    for dx in range(4):
        for dc in range(2):
            if dx or dc:
                pl.semaphore_signal(barrier, inc=1, device_id=dev(x_=(x + dx) % 4, c_=(c + dc) % 2), device_id_type=MESH)
    for core in range(2):
        pl.semaphore_signal(barrier, inc=1, device_id=dev(zlo_=1 - zlo, c_=core), device_id_type=MESH)
    for other in (dev(y_=yp), dev(y_=ym), dev(zh_=zp), dev(zh_=zm)):
        pl.semaphore_signal(barrier, inc=1, device_id=other, device_id_type=MESH)

    kb = lax.broadcasted_iota(jnp.int32, (4, TPD), 1) // BLOCK
    qb = lax.broadcasted_iota(jnp.int32, (4, TPD), 0)
    for r in range(2):
        m = bm[r]
        seen = jnp.where(kb == 0, m[:, 0:1], jnp.where(kb == 1, m[:, 1:2], jnp.where(kb == 2, m[:, 2:3], m[:, 3:4])))
        mk[8 * r : 8 * r + 4, :] = jnp.where(jnp.logical_or(seen > 0, kb == qb), 1.0, 0.0)
        mk[8 * r + 4 : 8 * r + 8, :] = jnp.zeros((4, TPD), jnp.float32)
    mbuf[x] = mk[...]

    pl.semaphore_wait(barrier, 13)

    def swap(e, p, w):
        src = w.at[:, pl.ds(e * NC, NC)]
        here = b_at(x, y, zh).at[:, pl.ds(p * NC, NC)]
        away = jnp.logical_or(c + 2 * e != x, x // 2 != c)
        far = remote(src, here, SW + e, SW + x % 2, dev(x_=c + 2 * e, c_=x // 2))
        return away, far, pltpu.make_async_copy(src, here, rsem.at[SW + x % 2])

    for e in range(2):
        for p, w in enumerate((wq, wk, wv)):
            away, far, near = swap(e, p, w)

            @pl.when(away)
            def _():
                far.start()

            @pl.when(jnp.logical_not(away))
            def _():
                near.start()

    load.wait()
    lane = lax.broadcasted_iota(jnp.int32, (64, 128), 1)

    def stats(i, _):
        rr = pl.multiple_of(i * 64, 64)
        t1 = jnp.zeros((64, 128), jnp.float32)
        t2 = jnp.zeros((64, 128), jnp.float32)
        for j in range(FEAT // 128):
            v = tv[pl.ds(rr, 64), j * 128 : (j + 1) * 128].astype(jnp.float32)
            t1 = t1 + v
            t2 = t2 + v * v
        a1 = jnp.sum(t1, axis=-1, keepdims=True)
        a2 = jnp.sum(t2, axis=-1, keepdims=True)
        st[pl.ds(rr, 64), :] = jnp.where(lane == 0, a1, jnp.where(lane == 1, a2, 0.0))
        return 0

    lax.fori_loop(0, 8, stats, 0)
    for i in range(4):
        sg[t, :, i * 128 : (i + 1) * 128] = jnp.transpose(st[i * 128 : (i + 1) * 128, :])[:8]

    peers = [dev(c_=1 - c), dev(zlo_=1 - zlo), dev(zlo_=1 - zlo, c_=1 - c)]
    for k in range(3):
        remote(sg.at[t], sg.at[t], ST + k, ST + k, peers[k]).start()
    for k in range(3):
        remote(mk, mbuf.at[x], MK + k, MK + k, dev(x_=(x + k + 1) % 4)).start()
    theirs = [t + 1 - 2 * c, (t + 2) % 4, (t + 2) % 4 + 1 - 2 * c]
    for k in range(3):
        got(sg.at[theirs[k]], ST + k)
    total = (sg[0] + sg[1]) + (sg[2] + sg[3])
    mean = total[0:1] * (1.0 / D)
    rstd = lax.rsqrt(total[1:2] * (1.0 / D) - mean * mean + EPS)
    row = lax.broadcasted_iota(jnp.int32, (128, 128), 0)
    for i in range(4):
        cols = slice(i * 128, (i + 1) * 128)
        st[i * 128 : (i + 1) * 128, :] = jnp.transpose(jnp.where(row == 0, mean[:, cols], rstd[:, cols]))

    def norm(i, _):
        rr = pl.multiple_of(i * 64, 64)
        mu = jnp.broadcast_to(st[pl.ds(rr, 64), 0:1], (64, 128))
        rs = jnp.broadcast_to(st[pl.ds(rr, 64), 1:2], (64, 128))
        for j in range(FEAT // 128):
            v = tv[pl.ds(rr, 64), j * 128 : (j + 1) * 128].astype(jnp.float32)
            g = gn[:, pl.ds(pl.multiple_of(t * FEAT + j * 128, 128), 128)]
            nv[pl.ds(rr, 64), j * 128 : (j + 1) * 128] = ((v - mu) * rs * g).astype(jnp.bfloat16)
        return 0

    def first(r, dst_dev, base):
        return remote(nv.at[pl.ds(pl.multiple_of(r * TPD, TPD), TPD), :], a_at(x, t), base + r, base + c, dst_dev)

    turns = [c, 1 - c]
    for r in turns:
        lax.fori_loop(r * 4, r * 4 + 4, norm, 0)
        first(r, dev(x_=xp, c_=r), AXP).start()
        first(r, dev(x_=xm, c_=r), AXM).start()
    half = nv.at[pl.ds(pl.multiple_of((1 - c) * TPD, TPD), TPD), :]
    remote(half, a_at(x, t), AD, AD, dev(c_=1 - c)).start()
    own = pltpu.make_async_copy(nv.at[pl.ds(pl.multiple_of(c * TPD, TPD), TPD), :], a_at(x, t), rsem.at[AL])
    own.start()

    xw = [2 * c, 2 * c + 1]
    names = [zh, zm, zp, zo]

    def y_out(k, h):
        piece = b_at(xw[h], y, names[k])
        relay(piece, YP + 2 * k + h, dev(y_=yp))
        relay(piece, YM + 2 * k + h, dev(y_=ym))
        relay(piece, DO + 2 * k + h, dev(c_=1 - c))

    def y_on(k, h):
        got(b_at(xw[h], ym, names[k]), YP + 2 * k + h)
        if h == 0:
            relay(b_at(xw[0], ym, names[k]), YFP + k, dev(y_=yp))
        got(b_at(xw[h], yp, names[k]), YM + 2 * k + h)
        if h == 1:
            relay(b_at(xw[1], yp, names[k]), YFM + k, dev(y_=ym))

    for h in range(2):
        piece = b_at(xw[h], y, zh)
        got(piece, SW + h)
        relay(piece, ZP + h, dev(zh_=zp))
        relay(piece, ZM + h, dev(zh_=zm))
        y_out(0, h)

    acc[...] = jnp.zeros_like(acc)

    near_q = [2 * zlo + c, 2 * zlo + 1 - c]
    far_q = [2 * (1 - zlo) + c, 2 * (1 - zlo) + 1 - c]
    MID = TPD // 2

    def pair_on(part, plus, minus, r0, rows):
        piece = a_at(x, far_q[part], r0, rows)
        relay(piece, plus, dev(x_=xp))
        relay(piece, minus, dev(x_=xm))

    def order(i):
        return (x + jnp.where(i == 1, 3, jnp.where(i == 2, 1, jnp.where(i == 3, 2, 0)))) % 4

    def chunk(xb, half, yy):
        row = pl.multiple_of(xb * TPD, TPD)
        at = [pl.ds(pl.multiple_of(((2 * half + k) * 4 + yy) * 4 * ROWS, 128), 4 * ROWS) for k in range(2)]
        acc[pl.ds(row, TPD), :] += jnp.dot(
            jnp.concatenate([a_buf[pl.ds(row, TPD), at[k]] for k in range(2)], axis=1),
            jnp.concatenate([b_buf[at[k], :] for k in range(2)], axis=0),
            preferred_element_type=jnp.float32,
        )

    def beside(i):
        return (y + jnp.where(i == 1, 3, jnp.where(i == 2, 1, 0))) % 4

    def early(i, _):
        chunk(order(i), zlo, y)
        return 0

    def middle(i, _):
        chunk(order(i // 2), zlo, beside(1 + i % 2))
        return 0

    def opposite(i, _):
        chunk(xo, zlo, beside(i))
        return 0

    def across(i, _):
        chunk(x, 1 - zlo, beside(i))
        return 0

    def late(i, _):
        chunk(order(jnp.where(i == 4, 0, i)), jnp.where(i == 4, 1 - zlo, zlo), yo)
        return 0

    xv = [2 * (1 - c), 2 * (1 - c) + 1]
    y_on(0, 0)
    got(b_at(xw[0], y, zm), ZP)
    relay(b_at(xw[0], y, zm), ZFP, dev(zh_=zp))
    y_out(1, 0)
    got(b_at(xw[0], y, zp), ZM)
    y_out(2, 0)
    y_on(0, 1)
    got(b_at(xw[1], y, zm), ZP + 1)
    y_out(1, 1)
    got(b_at(xw[1], y, zp), ZM + 1)
    relay(b_at(xw[1], y, zp), ZFM, dev(zh_=zm))
    y_out(2, 1)
    y_on(1, 0)
    y_on(2, 0)
    got(b_at(xw[0], y, zo), ZFP)
    for r in turns:
        first(r, dev(zlo_=1 - zlo, c_=r), AZ).start()
    y_out(3, 0)
    got(b_at(xw[1], y, zo), ZFM)
    y_out(3, 1)
    def ahead(part, plus, minus, core):
        got(a_at(xm, near_q[part]), AXP + core)
        relay(a_at(xm, near_q[part], 0, MID), plus, dev(x_=xp))
        got(a_at(xp, near_q[part]), AXM + core)
        relay(a_at(xp, near_q[part], MID, MID), minus, dev(x_=xm))

    ahead(0, AOP, AOM, c)
    y_on(1, 1)
    y_on(2, 1)
    ahead(1, AQP, AQM, 1 - c)
    for h in range(2):
        for k in range(4):
            got(b_at(xv[h], y, names[k]), DO + 2 * k + h)
    got(a_at(x, 2 * zlo + 1 - c), AD)
    own.wait()
    lax.fori_loop(0, 3, early, 0)
    got(a_at(x, far_q[0]), AZ + c)
    pair_on(0, AIIP, AIIM, 0, TPD)
    y_on(3, 0)
    y_on(3, 1)
    for base, yy in ((DYM, ym), (DYP, yp)):
        for h in range(2):
            relay(b_at(xw[h], yy, 0, 4), base + h, dev(c_=1 - c))
    got(a_at(xo, near_q[0], 0, MID), AOP)
    relay(a_at(xo, near_q[0], 0, BZ), AIII, dev(zlo_=1 - zlo))
    got(a_at(xo, near_q[1], 0, MID), AQP)
    relay(a_at(xo, near_q[1], 0, MID), AIII + 1, dev(zlo_=1 - zlo))
    got(a_at(xo, near_q[1], MID, MID), AQM)
    relay(a_at(xo, near_q[1], MID, MID), AIV, dev(zlo_=1 - zlo))
    for base, yy in ((DYM, ym), (DYP, yp)):
        for h in range(2):
            got(b_at(xv[h], yy, 0, 4), base + h)
    lax.fori_loop(0, 6, middle, 0)
    got(a_at(x, far_q[1]), AZ + 1 - c)
    pair_on(1, AIIP + 1, AIIM + 1, 0, MID)
    got(a_at(xo, near_q[0], MID, MID), AOM)
    lax.fori_loop(0, 3, opposite, 0)
    for h, num in enumerate((YFP, YFM)):
        for k in range(4):
            got(b_at(xw[h], yo, names[k]), num + k)
        relay(b_at(xw[h], yo, 0, 4), DYO + h, dev(c_=1 - c))
    got(a_at(xm, far_q[0]), AIIP)
    relay(a_at(xm, far_q[0], BZ, BP), AFP, dev(x_=xp))
    got(a_at(xp, far_q[0]), AIIM)
    relay(a_at(xp, far_q[0], BZ + BP, BM), AFM, dev(x_=xm))
    pair_on(1, ALP, ALM, MID, MID)
    lax.fori_loop(0, 3, across, 0)
    for h in range(2):
        got(b_at(xv[h], yo, 0, 4), DYO + h)
    lax.fori_loop(0, 5, late, 0)
    for k in range(3):
        got(mbuf.at[(x + 3 - k) % 4], MK + k)

    def unit(xb, q, r0=0, n=TPD):
        row = pl.multiple_of(xb * TPD + r0, MID)
        col = pl.multiple_of(q * FEAT, FEAT)
        acc[pl.ds(row, n), :] += jnp.dot(
            a_buf[pl.ds(row, n), pl.ds(col, FEAT)], b_buf[pl.ds(col, FEAT), :], preferred_element_type=jnp.float32
        )

    def out_copy(xb, i, j):
        src = obuf.at[i, :, pl.ds(j * DH, DH)]
        cols = pl.ds(pl.multiple_of((x // 2) * NC + j * DH, DH), DH)
        dst = out.at[pl.ds(pl.multiple_of(c * TPD, TPD), TPD), cols]
        rid = OUT + 2 * (x // 2) + c
        return remote(src, dst, OUT + i, rid, dev(x_=xb, c_=x % 2)), pltpu.make_async_copy(src, dst, rsem.at[rid])

    def goes(xb):
        return jnp.logical_or(xb != x, x % 2 != c)

    def finish(i):
        xb = order(i)
        row = pl.multiple_of(xb * TPD, TPD)

        def part(p, j):
            return acc[pl.ds(row, TPD), p * NC + j * DH : p * NC + (j + 1) * DH]

        def head_norm(values, gain):
            ms = jnp.mean(values * values, axis=-1, keepdims=True)
            return (values * lax.rsqrt(ms + EPS) * gain).astype(jnp.bfloat16)

        allowed = mbuf[xb]
        seen = jnp.concatenate(
            [jnp.broadcast_to(jnp.where(c == 0, allowed[b : b + 1], allowed[8 + b : 9 + b]), (BLOCK, TPD)) for b in range(4)], axis=0
        )
        for j in range(3):
            qn = head_norm(part(0, j), qg[...])
            kn = head_norm(part(1, j), kg[...])
            v = part(2, j).astype(jnp.bfloat16)
            s = lax.dot_general(qn, kn, (((1,), (1,)), ((), ())), preferred_element_type=jnp.float32) * (1.0 / DH**0.5)
            s = jnp.where(seen > 0, s, jnp.float32(-1e30))
            w = jnp.exp(s - jnp.max(s, axis=-1, keepdims=True))
            probs = (w / jnp.sum(w, axis=-1, keepdims=True)).astype(jnp.bfloat16)
            obuf[i, :, j * DH : (j + 1) * DH] = jnp.dot(probs, v, preferred_element_type=jnp.float32).astype(jnp.bfloat16)
            far, near_ = out_copy(xb, i, j)

            @pl.when(goes(xb))
            def _():
                far.start()

            @pl.when(jnp.logical_not(goes(xb)))
            def _():
                near_.start()

    finish(0)

    def third(i, _):
        @pl.when(i == 3)
        def _():
            got(a_at(xo, far_q[0], 0, BZ), AIII)
            got(a_at(xo, far_q[0], BZ, BP), AFP)
            got(a_at(xo, far_q[0], BZ + BP, BM), AFM)

        unit(order(i), far_q[0])
        return 0

    lax.fori_loop(1, 4, third, 0)

    def upper(i, _):
        for k, (num, blk) in enumerate(((AIIP, xm), (AIIM, xp))):

            @pl.when(i == k + 1)
            def _():
                got(a_at(blk, far_q[1], 0, MID), num + 1)

        unit(order(i), far_q[1], 0, MID)
        return 0

    lax.fori_loop(1, 3, upper, 0)

    got(a_at(xo, far_q[1], 0, MID), AIII + 1)
    got(a_at(xo, far_q[1], MID, MID), AIV)
    unit(xo, far_q[1])
    finish(3)

    def last(i, _):
        for k, (num, blk) in enumerate(((ALP, xm), (ALM, xp))):

            @pl.when(i == k + 1)
            def _():
                got(a_at(blk, far_q[1], MID, MID), num)

        unit(order(i), far_q[1], MID, MID)
        finish(i)
        return 0

    lax.fori_loop(1, 3, last, 0)

    for e in range(2):
        for r in range(2):
            got(out.at[pl.ds(r * TPD, TPD), pl.ds(e * NC, NC)], OUT + 2 * e + r)
    for num in (AXP, AXP + 1, AXM, AXM + 1, AD, AIIP, AIIM):
        sent(a_at(x, t), num)
    sent(a_at(x, t, 0, BZ), AIII)
    for num in (AOP, AOM, AQP, AQM, AIII + 1, AIV, AIIP + 1, AIIM + 1, ALP, ALM):
        sent(a_at(x, t, 0, MID), num)
    for r in range(2):
        sent(a_at(x, t), AZ + r)
    sent(a_at(x, t, 0, BP), AFP)
    sent(a_at(x, t, 0, BM), AFM)
    for k in range(3):
        sent(mk, MK + k)
        sent(sg.at[t], ST + k)
    for e in range(2):

        @pl.when(jnp.logical_or(c + 2 * e != x, x // 2 != c))
        def _():
            sent(b_at(x, y, zh), SW + e)

    for num in range(ZP, DYM):
        sent(b_at(x, y, zh), num)
    for num in range(DYM, OUT):
        sent(b_at(x, y, 0, 4), num)
    for i in range(4):

        @pl.when(goes(order(i)))
        def _():
            sent(obuf.at[i], OUT + i)


def per_device(tokens, block_mask, norm_gain, w_query, w_key, w_value, query_gain, key_gain):
    vmem = pl.BlockSpec(memory_space=pltpu.VMEM)
    hbm = pl.BlockSpec(memory_space=pl.ANY)
    return pl.pallas_call(
        kernel,
        out_shape=pltpu.VMEM((512, 768), jnp.bfloat16),
        in_specs=[hbm, vmem, vmem, hbm, hbm, hbm, vmem, vmem],
        out_specs=vmem,
        scratch_shapes=[
            pltpu.VMEM((2 * TPD, FEAT), jnp.bfloat16),
            pltpu.VMEM((2 * TPD, FEAT), jnp.bfloat16),
            pltpu.VMEM((2 * TPD, 128), jnp.float32),
            pltpu.VMEM((4, 8, 2 * TPD), jnp.float32),
            pltpu.VMEM((4 * TPD, D), jnp.bfloat16),
            pltpu.VMEM((D, N), jnp.bfloat16),
            pltpu.VMEM((4 * TPD, N), jnp.float32),
            pltpu.VMEM((16, TPD), jnp.float32),
            pltpu.VMEM((4, 16, TPD), jnp.float32),
            pltpu.VMEM((4, TPD, NC), jnp.bfloat16),
            pltpu.SemaphoreType.DMA((COUNT,)),
            pltpu.SemaphoreType.DMA((COUNT,)),
        ],
        compiler_params=pltpu.CompilerParams(collective_id=0, has_side_effects=True, vmem_limit_bytes=60 << 20),
    )(tokens, block_mask, norm_gain.reshape(1, D), w_query, w_key, w_value, query_gain.reshape(1, DH), key_gain.reshape(1, DH))


def solution(mesh):
    return jax.shard_map(
        per_device,
        mesh=mesh,
        in_specs=(
            P("dp", "tensor"),
            P("dp", None, None),
            P(),
            P("dp", "tensor"),
            P("dp", "tensor"),
            P("dp", "tensor"),
            P(),
            P(),
        ),
        out_specs=P("dp", "tensor"),
        check_vma=False,
    )
```
